256 devices in a mesh: ctx: 64 (over z, x, core), fsdp: 4 (over y).
Axes of the slice: x: 4, y: 4, z: 8, core: 2. Of those that a mesh axis runs over, the one named last changes fastest.
Arguments:
- queries: bfloat16 [8192, 2048], P('ctx', 'fsdp'), may hold values from -120 to 120
- keys: bfloat16 [8192, 256], P('ctx'), may hold values from -5 to 5
- values: bfloat16 [8192, 256], P('ctx'), may hold values from -5 to 5
- out_grad: bfloat16 [8192, 2048], P('ctx', 'fsdp'), may hold values from -5 to 5
- hidden: bfloat16 [8192, 8192], P('ctx', 'fsdp'), may hold values from -40 to 40
- key_weight: bfloat16 [8192, 256], P('fsdp'), may hold values from -10 to 10
- value_weight: bfloat16 [8192, 256], P('fsdp'), may hold values from -10 to 10
- stretch_owner: int32 [64], replicated, may hold values from 0 to 63, as said below
- positions: int32 [8192], P('ctx'), may hold values from 0 to 4095, as said below
Outputs:
- query_grad: bfloat16 [8192, 2048], P('ctx', 'fsdp')
- key_weight_grad: float32 [8192, 256], P('fsdp')
- value_weight_grad: float32 [8192, 256], P('fsdp')
The draws below stay inside these ranges and needn't reach their ends.
Inputs may be any that keep to these rules, and one draw needn't show every extreme that they name: A permutation; index b of ctx holds sequence stretch stretch_owner[b] in its first 64 rows and stretch 2 * 64 - 1 - stretch_owner[b] in the others. `positions`: documents are contiguous in sequence order; a row's position counts from its document's first token, and the sequence's first token has position 0.
All inputs are finite; a program needn't handle non-finite values.
Results may differ from the reference program's by a relative error of at most 0.015.
Values may be sent and summed in bfloat16 or wider, within the bound.
A program may use at most 64 MiB of HBM per device.

```python
import math
import jax
import jax.numpy as jnp
from jax import lax

D = 8192
DH = 128
HPG = 8
KVG = 2
TOK_DEV = 128
TOKENS = 8192
HEADS = 16
PAIRS = 64


def draw_stretch_owner(key, part):
    return jax.random.permutation(jax.random.fold_in(key, 7), PAIRS).astype(jnp.int32)


def sequence_positions(key):
    span = TOKENS // 2
    begin = jax.random.randint(jax.random.fold_in(key, 31), (), 0, TOKENS - span + 1)
    index = jnp.arange(TOKENS, dtype=jnp.int32)
    starts = jax.random.randint(jax.random.fold_in(key, 32), (TOKENS,), 0, 256) == 0
    inside = (index >= begin) & (index < begin + span)
    starts = starts & jnp.logical_not(inside) | (index == begin) | (index == begin + span) | (index == 0)
    marks = jnp.where(starts, index, 0)
    last = lax.cummax(marks, axis=0)
    return (index - last).astype(jnp.int32)


def layout_rows(key):
    owners = draw_stretch_owner(key, 0)
    half = TOK_DEV // 2
    stretches = jnp.stack([owners, 2 * PAIRS - 1 - owners], axis=1)
    offsets = jnp.arange(half, dtype=jnp.int32)
    return (stretches[:, :, None] * half + offsets[None, None, :]).reshape(TOKENS)


def draw_positions(key, part):
    return sequence_positions(key)[layout_rows(key)].astype(jnp.int32)


def attention_pair(key):
    keys = jnp.clip(jax.random.normal(jax.random.fold_in(key, 41), (TOKENS, KVG * DH), jnp.float32), -5.0, 5.0)
    queries = jnp.clip(jax.random.normal(jax.random.fold_in(key, 42), (TOKENS, KVG * HPG * DH), jnp.float32), -5.0, 5.0)
    return (queries, keys)


def draw_queries(key, part):
    return attention_pair(key)[0].astype(jnp.bfloat16)


def draw_keys(key, part):
    return attention_pair(key)[1].astype(jnp.bfloat16)


def draw_hidden(key, part):
    rows = jnp.arange(TOKENS, dtype=jnp.float32)[:, None] / (TOKENS - 1)
    cols = jnp.arange(D, dtype=jnp.float32)[None, :] / (D - 1)
    gain = jnp.exp(jax.random.uniform(jax.random.fold_in(key, 51), (1, D), jnp.float32, math.log(0.03), math.log(0.3)))
    base = jnp.clip(jax.random.normal(jax.random.fold_in(key, 52), (TOKENS, D), jnp.float32), -5.0, 5.0)
    ramp = (1.0 + 2.0 * rows) * (3.0 - 2.0 * cols)
    return (base * gain * ramp).astype(jnp.bfloat16)


def weight_law(key, salt):
    cols = jnp.exp(jax.random.uniform(jax.random.fold_in(key, salt), (1, KVG * DH), jnp.float32, math.log(0.1), math.log(10.0)))
    rows = 1.0 + 2.0 * jnp.arange(D, dtype=jnp.float32)[:, None] / (D - 1)
    base = jnp.clip(jax.random.normal(jax.random.fold_in(key, salt + 1), (D, KVG * DH), jnp.float32), -5.0, 5.0)
    return base * rows * cols / math.sqrt(D)


def draw_key_weight(key, part):
    return weight_law(key, 61).astype(jnp.bfloat16)


def draw_value_weight(key, part):
    return weight_law(key, 71).astype(jnp.bfloat16)


def levels(stream_key, shape, shards, least, high):
    level = 1.0
    for axis_at, parts in shards:
        heights = jax.random.uniform(jax.random.fold_in(jax.random.fold_in(stream_key, 6), axis_at), (parts,), jnp.float32, least / len(shards), high / len(shards))
        level = level * jnp.repeat(jnp.exp(heights), shape[axis_at] // parts).reshape((-1,) + (1,) * (len(shape) - 1 - axis_at))
    return level


def bell_draw(rng, shape, deviation, limit, pieces=(), kind=jnp.bfloat16):
    array = jax.random.normal(rng, shape, jnp.float32) * deviation
    if len(pieces) > 0:
        array = levels(rng, shape, pieces, -0.22, 0.18) * array
    return jnp.clip(array, min=-limit, max=limit).astype(kind)


def setup_inputs(seed: int = 0) -> dict:
    arg_keys = jax.random.split(jax.random.key(seed), 10)
    return {
        "queries": draw_queries(jax.random.fold_in(arg_keys[9], 71), 0),
        "keys": draw_keys(jax.random.fold_in(arg_keys[9], 71), 0),
        "values": bell_draw(arg_keys[2], (TOKENS, KVG * DH), 1.0, 5.0, ((0, 64),)),
        "out_grad": bell_draw(arg_keys[3], (TOKENS, HEADS * DH), 1.0, 5.0, ((0, 64), (1, 4))),
        "hidden": draw_hidden(jax.random.fold_in(arg_keys[9], 71), 0),
        "key_weight": draw_key_weight(jax.random.fold_in(arg_keys[9], 71), 0),
        "value_weight": draw_value_weight(jax.random.fold_in(arg_keys[9], 71), 0),
        "stretch_owner": draw_stretch_owner(jax.random.fold_in(arg_keys[9], 71), 0),
        "positions": draw_positions(jax.random.fold_in(arg_keys[9], 71), 0),
    }


CLIP_RATE = 0.02
EPSILON = 1e-06
NEGATIVE = -1e+30

def head_grads(query_head, grad_head, key_group, value_group, place, floor):
    scale = 1.0 / math.sqrt(DH)
    block = min(512, TOKENS)

    def step(carry, index):
        key_acc, value_acc = carry
        start = index * block
        q_block = lax.dynamic_slice_in_dim(query_head, start, block, 0)
        g_block = lax.dynamic_slice_in_dim(grad_head, start, block, 0)
        q_place = lax.dynamic_slice_in_dim(place, start, block, 0)
        q_floor = lax.dynamic_slice_in_dim(floor, start, block, 0)
        seen = (place[None, :] <= q_place[:, None]) & (place[None, :] >= q_floor[:, None])
        raw = jnp.dot(q_block, key_group.T, precision=lax.Precision.HIGHEST) * scale
        scores = jnp.where(seen, raw, NEGATIVE)
        top = lax.optimization_barrier(jnp.max(scores, axis=1))
        mass = lax.optimization_barrier(jnp.sum(jnp.where(seen, jnp.exp(scores - top[:, None]), 0.0), axis=1))
        lse = top + jnp.log(mass)
        probs = jnp.where(seen, jnp.exp(scores - lse[:, None]), 0.0)
        dprobs = jnp.dot(g_block, value_group.T, precision=lax.Precision.HIGHEST)
        delta = lax.optimization_barrier(jnp.sum(probs * dprobs, axis=1))
        slopes = (probs * (dprobs - delta[:, None]) * scale).astype(jnp.bfloat16)
        slopes = lax.optimization_barrier(slopes).astype(jnp.float32)
        probs_b = lax.optimization_barrier(probs.astype(jnp.bfloat16)).astype(jnp.float32)
        query_part = jnp.dot(slopes, key_group, precision=lax.Precision.HIGHEST).astype(jnp.bfloat16)
        key_acc = key_acc + jnp.dot(slopes.T, q_block, precision=lax.Precision.HIGHEST)
        value_acc = value_acc + jnp.dot(probs_b.T, g_block, precision=lax.Precision.HIGHEST)
        return ((key_acc, value_acc), query_part)
    zero = jnp.zeros((TOKENS, DH), jnp.float32)
    (key_acc, value_acc), query_parts = lax.scan(step, (zero, zero), jnp.arange(TOKENS // block))
    return (key_acc, value_acc, query_parts.reshape(TOKENS, DH))

def reference(queries, keys, values, out_grad, hidden, key_weight, value_weight, stretch_owner, positions):
    half = TOK_DEV // 2
    owners = stretch_owner.astype(jnp.int32)
    stretches = jnp.stack([owners, 2 * PAIRS - 1 - owners], axis=1)
    offsets = jnp.arange(half, dtype=jnp.int32)
    place = (stretches[:, :, None] * half + offsets[None, None, :]).reshape(TOKENS).astype(jnp.int32)
    floor = place - positions.astype(jnp.int32)
    query_all = queries.astype(jnp.float32)
    grad_all = out_grad.astype(jnp.float32)
    key_parts = []
    value_parts = []
    query_parts = []
    for group in range(KVG):
        key_group = keys[:, group * DH:(group + 1) * DH].astype(jnp.float32)
        value_group = values[:, group * DH:(group + 1) * DH].astype(jnp.float32)
        key_acc = jnp.zeros((TOKENS, DH), jnp.float32)
        value_acc = jnp.zeros((TOKENS, DH), jnp.float32)
        for member in range(HPG):
            head = group * HPG + member
            key_term, value_term, query_part = head_grads(query_all[:, head * DH:(head + 1) * DH], grad_all[:, head * DH:(head + 1) * DH], key_group, value_group, place, floor)
            key_acc = key_acc + key_term
            value_acc = value_acc + value_term
            query_parts.append(query_part)
        key_parts.append(key_acc)
        value_parts.append(value_acc)
    query_grad = jnp.concatenate(query_parts, axis=1)
    key_grads = jnp.concatenate(key_parts, axis=1).astype(jnp.bfloat16)
    value_grads = jnp.concatenate(value_parts, axis=1).astype(jnp.bfloat16)
    raw_key = jnp.dot(hidden.T, key_grads, preferred_element_type=jnp.float32)
    raw_value = jnp.dot(hidden.T, value_grads, preferred_element_type=jnp.float32)
    key_f = key_weight.astype(jnp.float32)
    value_f = value_weight.astype(jnp.float32)

    def clip(raw, weight):
        weight_norm = jnp.sqrt(lax.optimization_barrier(jnp.sum(weight * weight, axis=0)) + EPSILON)
        grad_norm = jnp.sqrt(lax.optimization_barrier(jnp.sum(raw * raw, axis=0)) + EPSILON)
        factor = jnp.minimum(1.0, CLIP_RATE * TOKENS * weight_norm / grad_norm)
        return raw * factor[None, :]
    return (query_grad, clip(raw_key, key_f), clip(raw_value, value_f))
```

```python
import functools
import math

import jax
import jax.numpy as jnp
from jax import lax
from jax.experimental import pallas as pl
from jax.experimental.pallas import tpu as pltpu
from jax.sharding import PartitionSpec as P

DH = 128
HPG = 8
KVG = 2
TOK = 128
HALF = TOK // 2
Z = 8
X = 4
C = 2
Y = 4
G = X * C
PAIRS = Z * X * C
HEADS = 4
ROWS = G * TOK
CLIP_RATE = 0.02
EPSILON = 1e-06
NEGATIVE = -1e30
SCALE = 1.0 / math.sqrt(DH)
SCALE2 = SCALE * math.log2(math.e)
MESH = pl.DeviceIdType.MESH
ANY = pl.BlockSpec(memory_space=pl.ANY)
VMEM = pl.BlockSpec(memory_space=pltpu.VMEM)
SMEM = pl.BlockSpec(memory_space=pltpu.SMEM)
LAST = (((1,), (1,)), ((), ()))
FIRST = (((0,), (0,)), ((), ()))
BF16 = jnp.bfloat16
F32 = jnp.float32


class Place:
    def __init__(self):
        me = lax.axis_index("ctx")
        self.me = me
        self.y = lax.axis_index("fsdp")
        self.z = lax.div(me, G)
        self.slot = lax.rem(me, G)
        self.x = lax.div(self.slot, C)
        self.c = lax.rem(self.slot, C)

    def xslot(self, step, flip=False):
        x = lax.rem(self.x + step + X, X)
        return x * C + ((1 - self.c) if flip else self.c)

    def in_plane(self, slot):
        return {"ctx": self.z * G + slot}

    def zslot(self, step):
        return lax.rem(self.z + step + Z, Z)

    def in_column(self, z):
        return {"ctx": z * G + self.slot}

    def yslot(self, step):
        return lax.rem(self.y + step, Y)


class Copies:
    def __init__(self, send, recv):
        self.send, self.recv, self.made = send, recv, []

    def __call__(self, src, dst, device):
        i = len(self.made)
        copy = pltpu.make_async_remote_copy(
            src_ref=src,
            dst_ref=dst,
            send_sem=self.send.at[i],
            recv_sem=self.recv.at[i],
            device_id=device,
            device_id_type=MESH,
        )
        copy.start()
        self.made.append(copy)
        return copy

    def wait_sends(self):
        for copy in self.made:
            copy.wait_send()


def barrier(devices):
    sem = pltpu.get_barrier_semaphore()
    for device in devices:
        pl.semaphore_signal(sem, inc=1, device_id=device, device_id_type=MESH)
    pl.semaphore_wait(sem, len(devices))


def at(slot, rows, offset=0, count=None):
    return pl.ds(pl.multiple_of(slot * rows + offset, 16), rows if count is None else count)


def plane_ring(copies, p, src, out, rows):
    half = rows // 2
    right, left = p.xslot(1), p.xslot(-1)
    far = p.xslot(2)
    partner = p.in_plane(p.xslot(0, True))
    mine = out.at[at(p.slot, rows)]
    a = copies(src, mine, p.in_plane(right))
    b = copies(src, mine, p.in_plane(left))
    own = copies(src, mine, partner)
    yield
    a.wait_recv()
    first = out.at[at(left, rows, 0, half)]
    f = copies(first, first, p.in_plane(right))
    block = out.at[at(left, rows)]
    pa = copies(block, block, partner)
    b.wait_recv()
    second = out.at[at(right, rows, half, half)]
    g = copies(second, second, p.in_plane(left))
    block = out.at[at(right, rows)]
    pb = copies(block, block, partner)
    yield
    f.wait_recv()
    g.wait_recv()
    block = out.at[at(far, rows)]
    pc = copies(block, block, partner)
    yield
    own.wait_recv()
    pa.wait_recv()
    pb.wait_recv()
    pc.wait_recv()


def column_ring(copies, p, src, where):
    up, down = p.in_column(p.zslot(1)), p.in_column(p.zslot(-1))
    u = copies(src, where(p.z), up)
    d = copies(src, where(p.z), down)
    for step in range(1, Z // 2 + 1):
        yield
        u.wait_recv()
        if step < Z // 2:
            block = where(p.zslot(-step))
            u = copies(block, block, up)
        if step < Z // 2:
            d.wait_recv()
            if step < Z // 2 - 1:
                block = where(p.zslot(step))
                d = copies(block, block, down)


def run(*rings):
    rings = list(rings)
    while rings:
        rings = [ring for ring in rings if next(ring, True) is None]


def plane_peers(p):
    return [p.in_plane(p.xslot(s, f)) for s in range(X) for f in (False, True) if s or f]


def column_peers(p):
    return [p.in_column(p.zslot(s)) for s in range(1, Z)]


def row_peers(p):
    return [{"fsdp": p.yslot(s)} for s in range(1, Y)]


def gather_kernel(
    q, do, k, v, hid, pos, qg, dog, kg, vg, hg, pg, tq, tdo, tk, tv, th, tp, send, recv, local
):
    p = Place()
    group = lax.div(p.y * HEADS, HPG)
    cols = pl.ds(pl.multiple_of(group * DH, DH), DH)
    wide = hid.shape[1] // G
    own_hid = hid.at[:, pl.ds(pl.multiple_of(p.slot * wide, 128), wide)]
    own_k, own_v = k.at[:, cols], v.at[:, cols]
    mine = at(p.slot, TOK)
    moves = [
        (q, tq, qg.at[mine]),
        (do, tdo, dog.at[mine]),
        (own_k, tk, kg.at[at(p.z, TOK)]),
        (own_v, tv, vg.at[at(p.z, TOK)]),
        (own_hid, th, hg.at[mine]),
        (pos, tp, pg.at[p.slot]),
    ]
    loads = [pltpu.make_async_copy(s, t, local.at[i]) for i, (s, t, _) in enumerate(moves)]
    for load in loads:
        load.start()
    barrier(plane_peers(p) + [p.in_column(p.zslot(1)), p.in_column(p.zslot(-1))])
    copies = Copies(send, recv)
    rings = [
        column_ring(copies, p, own_k, lambda z: kg.at[at(z, TOK)]),
        plane_ring(copies, p, q, qg, TOK),
        column_ring(copies, p, own_v, lambda z: vg.at[at(z, TOK)]),
        plane_ring(copies, p, do, dog, TOK),
    ]
    for ring in rings:
        next(ring)
    stores = []
    for i, (_, t, d) in enumerate(moves):
        loads[i].wait()
        store = pltpu.make_async_copy(t, d, local.at[len(moves) + i])
        store.start()
        stores.append(store)
    small = []
    for s in range(X):
        for f in (False, True):
            if s or f:
                to = p.xslot(s, f)
                small.append(copies(pos, pg.at[p.slot], p.in_plane(to)))
    next(rings[0])
    next(rings[2])
    next(rings[1])
    next(rings[3])
    for s in range(X):
        for f in (False, True):
            if s or f:
                to = p.xslot(s, f)
                part = hid.at[:, pl.ds(pl.multiple_of(to * wide, 128), wide)]
                small.append(copies(part, hg.at[mine], p.in_plane(to)))
    run(*rings)
    for copy in small:
        copy.wait_recv()
    copies.wait_sends()
    for store in stores:
        store.wait()


def tile_bias(owners, pos, bias, j, p, width):
    lane = lax.broadcasted_iota(jnp.int32, (1, TOK), 1)
    low = lane < HALF
    places, floors = [], []
    for s in range(width // TOK):
        slot = j * (width // TOK) + s
        owner = owners[p.z * G + slot]
        place = lane + jnp.where(low, owner * HALF, (2 * PAIRS - 1 - owner) * HALF - HALF)
        places.append(place)
        floors.append(place - pos[slot, 0:1, :])
    place = jnp.concatenate(places, axis=1)
    floor = jnp.concatenate(floors, axis=1)
    row = lax.broadcasted_iota(jnp.int32, (HALF, width), 0)
    for z in range(Z):
        owner = owners[z * G + p.slot]
        for h, stretch in enumerate((owner, 2 * PAIRS - 1 - owner)):
            key = row + stretch * HALF
            seen = (key <= place) & (key >= floor)
            bias[pl.ds(z * TOK + h * HALF, HALF), :] = jnp.where(seen, 0.0, NEGATIVE)


def stats_kernel(owners, pos, q, do, k, v, out, bias):
    p = Place()
    width = q.shape[0]
    tile_bias(owners, pos, bias, pl.program_id(0), p, width)
    for h in range(HEADS):
        cols = pl.ds(h * DH, DH)
        raw = lax.dot_general(k[...], q[:, cols], LAST, preferred_element_type=F32) + bias[...]
        top = jnp.max(raw, axis=0, keepdims=True)
        mass = jnp.exp2((raw - top) * SCALE2)
        total = jnp.sum(mass, axis=0, keepdims=True)
        dp = lax.dot_general(v[...], do[:, cols], LAST, preferred_element_type=F32)
        dsum = jnp.sum(mass * dp, axis=0, keepdims=True)
        out[h : h + 1, :] = top * SCALE2 + jnp.log2(total)
        out[HEADS + h : HEADS + h + 1, :] = dsum / total


def share_kernel(stats, out, send, recv, local):
    p = Place()
    load = pltpu.make_async_copy(stats, out.at[p.slot], local.at[0])
    load.start()
    barrier(plane_peers(p))
    copies = Copies(send, recv)
    made = [copies(stats, out.at[p.slot], peer) for peer in plane_peers(p)]
    for copy in made:
        copy.wait_recv()
    copies.wait_sends()
    load.wait()


def grads_kernel(owners, pos, stats, q, do, k, v, dq, dkv, bias, kt, probs, slopes, acc):
    p = Place()
    j = pl.program_id(0)
    width = q.shape[0]

    @pl.when(j == 0)
    def _():
        kt[...] = k[...].T
        acc[...] = jnp.zeros_like(acc)

    tile_bias(owners, pos, bias, j, p, width)
    for h in range(HEADS):
        cols = pl.ds(h * DH, DH)
        parts = stats[:, h, :]
        top = jnp.max(parts, axis=0, keepdims=True)
        weight = jnp.exp2(parts - top)
        total = jnp.sum(weight, axis=0, keepdims=True)
        lse = top + jnp.log2(total)
        delta = jnp.sum(weight * stats[:, HEADS + h, :], axis=0, keepdims=True) / total
        raw = lax.dot_general(k[...], q[:, cols], LAST, preferred_element_type=F32) + bias[...]
        prob = jnp.exp2(raw * SCALE2 - lse)
        dp = lax.dot_general(v[...], do[:, cols], LAST, preferred_element_type=F32)
        slope = (prob * (dp - delta)).astype(BF16)
        at_h = pl.ds(h * width, width)
        probs[:, at_h] = prob.astype(BF16)
        slopes[:, at_h] = slope
        dqt = jnp.dot(kt[...], slopes[:, at_h], preferred_element_type=F32)
        dq[:, cols] = (dqt * SCALE).T.astype(BF16)
    tall = lambda ref: jnp.concatenate([ref[:, pl.ds(h * DH, DH)] for h in range(HEADS)], axis=0)
    acc[:, :DH] += jnp.dot(slopes[...], tall(q), preferred_element_type=F32)
    acc[:, DH:] += jnp.dot(probs[...], tall(do), preferred_element_type=F32)

    @pl.when(j == pl.num_programs(0) - 1)
    def _():
        dkv[:, :DH] = (acc[:, :DH] * SCALE).astype(BF16)
        dkv[:, DH:] = acc[:, DH:].astype(BF16)


def reduce_kernel(dq, dkv, dq_slots, grads, tq, gz, ysend, gy, both, send, recv, local):
    p = Place()
    own_q = pltpu.make_async_copy(dq.at[at(p.slot, TOK)], tq, local.at[0])
    own_q.start()
    own_g = pltpu.make_async_copy(dkv.at[at(p.z, TOK)], gz.at[p.z], local.at[1])
    own_g.start()
    barrier(
        plane_peers(p) + column_peers(p) + row_peers(p)
    )
    copies = Copies(send, recv)
    zs = [
        copies(dkv.at[at(p.zslot(s), TOK)], gz.at[p.z], p.in_column(p.zslot(s)))
        for s in (4, 3, 5, 2, 6, 1, 7)
    ]
    qs = []
    for s, f in ((2, False), (2, True), (1, False), (3, False), (1, True), (3, True), (0, True)):
        to = p.xslot(s, f)
        qs.append(copies(dq.at[at(to, TOK)], dq_slots.at[p.slot], p.in_plane(to)))
    own_q.wait()
    put_q = pltpu.make_async_copy(tq, dq_slots.at[p.slot], local.at[2])
    put_q.start()
    own_g.wait()
    for copy in zs:
        copy.wait_recv()
    total = gz[0].astype(F32)
    for z in range(1, Z):
        total = total + gz[z].astype(F32)
    ysend[...] = total.astype(BF16)
    gy[p.y] = total.astype(BF16)
    ys = [copies(ysend, gy.at[p.y], peer) for peer in row_peers(p)]
    for copy in ys:
        copy.wait_recv()
    members = Y // KVG
    for g in range(KVG):
        part = gy[g * members].astype(F32)
        for i in range(1, members):
            part = part + gy[g * members + i].astype(F32)
        both[:, g * DH : (g + 1) * DH] = part[:, :DH].astype(BF16)
        both[:, (KVG + g) * DH : (KVG + g + 1) * DH] = part[:, DH:].astype(BF16)
    put_g = pltpu.make_async_copy(both, grads.at[at(p.slot, TOK)], local.at[3])
    put_g.start()
    run(plane_ring(copies, p, both, grads, TOK))
    for copy in qs:
        copy.wait_recv()
    copies.wait_sends()
    put_q.wait()
    put_g.wait()


def finish_kernel(part, weights, raw, sums, rz, buf, send, recv, local):
    p = Place()
    rows = part.shape[0]
    piece = rows // Z
    own = pltpu.make_async_copy(part.at[at(p.z, piece)], rz.at[p.z], local.at[0])
    own.start()
    barrier(plane_peers(p) + column_peers(p) + row_peers(p))
    copies = Copies(send, recv)
    zs = [
        copies(part.at[at(p.zslot(s), piece)], rz.at[p.z], p.in_column(p.zslot(s)))
        for s in (4, 3, 5, 2, 6, 1, 7)
    ]
    own.wait()
    for copy in zs:
        copy.wait_recv()
    total = rz[0].astype(F32)
    for z in range(1, Z):
        total = total + rz[z].astype(F32)
    where = lambda z: buf.at[pl.ds(pl.multiple_of(p.slot * rows + z * piece, 16), piece)]
    mine = pl.ds(pl.multiple_of(p.slot * rows + p.z * piece, 16), piece)
    buf[mine, :] = total.astype(BF16)
    run(column_ring(copies, p, where(p.z), where))
    run(plane_ring(copies, p, buf.at[at(p.slot, rows)], buf, rows))
    put = pltpu.make_async_copy(buf, raw, local.at[1])
    put.start()
    width = buf.shape[1]

    def step(i, acc):
        block = buf[pl.ds(pl.multiple_of(i * 64, 64), 64), :].astype(F32)
        return acc + jnp.sum((block * block).reshape(8, 8, width), axis=0)

    acc = lax.fori_loop(0, buf.shape[0] // 64, step, jnp.zeros((8, width), F32))
    row = lax.broadcasted_iota(jnp.int32, (8, width), 0)
    sums[p.y] = jnp.where(row == 0, jnp.sum(acc, axis=0, keepdims=True), weights[...])
    ys = [copies(sums.at[p.y], sums.at[p.y], peer) for peer in row_peers(p)]
    for copy in ys:
        copy.wait_recv()
    copies.wait_sends()
    put.wait()


def remote(ident, kernel, **kw):
    return pl.pallas_call(
        kernel,
        compiler_params=pltpu.CompilerParams(
            collective_id=ident, has_side_effects=True, vmem_limit_bytes=40 * 1024 * 1024
        ),
        **kw,
    )


def shape(dims, kind=BF16):
    return jax.ShapeDtypeStruct(dims, kind)


def dma(n):
    return pltpu.SemaphoreType.DMA((n,))


def local(
    queries, keys, values, out_grad, hidden, key_weight, value_weight, stretch_owner, positions
):
    width = queries.shape[1]
    model = hidden.shape[1]
    piece = model // G
    columns = KVG * DH
    pos = jnp.broadcast_to(positions[None, :], (8, TOK))
    qg, dog, kg, vg, hg, pg = remote(
        0,
        gather_kernel,
        out_shape=(
            shape((ROWS, width)),
            shape((ROWS, width)),
            shape((Z * TOK, DH)),
            shape((Z * TOK, DH)),
            shape((ROWS, piece)),
            shape((G, 8, TOK), jnp.int32),
        ),
        in_specs=[ANY] * 6,
        out_specs=(ANY,) * 6,
        scratch_shapes=[
            pltpu.VMEM((TOK, width), BF16),
            pltpu.VMEM((TOK, width), BF16),
            pltpu.VMEM((TOK, DH), BF16),
            pltpu.VMEM((TOK, DH), BF16),
            pltpu.VMEM((TOK, piece), BF16),
            pltpu.VMEM((8, TOK), jnp.int32),
            dma(64),
            dma(64),
            dma(12),
        ],
    )(queries, out_grad, keys, values, hidden, pos)
    tile = 256
    q_spec = pl.BlockSpec((tile, width), lambda j: (j, 0))
    k_spec = pl.BlockSpec((Z * TOK, DH), lambda j: (0, 0))
    pos_spec = pl.BlockSpec((G, 8, TOK), lambda j: (0, 0, 0))
    params = pltpu.CompilerParams(
        dimension_semantics=("arbitrary",), vmem_limit_bytes=48 * 1024 * 1024
    )
    stats = pl.pallas_call(
        stats_kernel,
        grid=(ROWS // tile,),
        out_shape=shape((2 * HEADS, ROWS), F32),
        in_specs=[SMEM, pos_spec, q_spec, q_spec, k_spec, k_spec],
        out_specs=pl.BlockSpec((2 * HEADS, tile), lambda j: (0, j)),
        scratch_shapes=[pltpu.VMEM((Z * TOK, tile), F32)],
        compiler_params=params,
    )(stretch_owner, pg, qg, dog, kg, vg)
    shared = remote(
        1,
        share_kernel,
        out_shape=shape((G, 2 * HEADS, ROWS), F32),
        in_specs=[VMEM],
        out_specs=VMEM,
        scratch_shapes=[dma(8), dma(8), dma(1)],
    )(stats)
    dq, dkv = pl.pallas_call(
        grads_kernel,
        grid=(ROWS // tile,),
        out_shape=(shape((ROWS, width)), shape((Z * TOK, 2 * DH))),
        in_specs=[
            SMEM,
            pos_spec,
            pl.BlockSpec((G, 2 * HEADS, tile), lambda j: (0, 0, j)),
            q_spec,
            q_spec,
            k_spec,
            k_spec,
        ],
        out_specs=(q_spec, pl.BlockSpec((Z * TOK, 2 * DH), lambda j: (0, 0))),
        scratch_shapes=[
            pltpu.VMEM((Z * TOK, tile), F32),
            pltpu.VMEM((DH, Z * TOK), BF16),
            pltpu.VMEM((Z * TOK, HEADS * tile), BF16),
            pltpu.VMEM((Z * TOK, HEADS * tile), BF16),
            pltpu.VMEM((Z * TOK, 2 * DH), F32),
        ],
        compiler_params=params,
    )(stretch_owner, pg, shared, qg, dog, kg, vg)
    dq_slots, grads = remote(
        2,
        reduce_kernel,
        out_shape=(shape((G, TOK, width)), shape((ROWS, 2 * columns))),
        in_specs=[ANY, ANY],
        out_specs=(ANY, ANY),
        scratch_shapes=[
            pltpu.VMEM((TOK, width), BF16),
            pltpu.VMEM((Z, TOK, 2 * DH), BF16),
            pltpu.VMEM((TOK, 2 * DH), BF16),
            pltpu.VMEM((Y, TOK, 2 * DH), BF16),
            pltpu.VMEM((TOK, 2 * columns), BF16),
            dma(40),
            dma(40),
            dma(4),
        ],
    )(dq, dkv)
    query_grad = jnp.sum(dq_slots.astype(F32), axis=0).astype(BF16)
    part = lax.dot_general(hg, grads, FIRST, preferred_element_type=F32).astype(BF16)
    key_f = key_weight.astype(F32)
    value_f = value_weight.astype(F32)
    weight_sq = jnp.concatenate([jnp.sum(key_f * key_f, axis=0), jnp.sum(value_f * value_f, axis=0)])
    raw, sums = remote(
        3,
        finish_kernel,
        out_shape=(shape((model, 2 * columns)), shape((Y, 8, 2 * columns), F32)),
        in_specs=[ANY, VMEM],
        out_specs=(ANY, VMEM),
        scratch_shapes=[
            pltpu.VMEM((Z, piece // Z, 2 * columns), BF16),
            pltpu.VMEM((model, 2 * columns), BF16),
            dma(40),
            dma(40),
            dma(2),
        ],
    )(part, jnp.broadcast_to(weight_sq[None, :], (8, 2 * columns)))
    total = jnp.sum(sums, axis=0)
    grad_norm = jnp.sqrt(total[0] + EPSILON)
    weight_norm = jnp.sqrt(total[1] + EPSILON)
    tokens = TOK * PAIRS
    factor = jnp.minimum(1.0, CLIP_RATE * tokens * weight_norm / grad_norm)
    key_out = raw[:, :columns].astype(F32) * factor[None, :columns]
    value_out = raw[:, columns:].astype(F32) * factor[None, columns:]
    return (query_grad, key_out, value_out)


def solution(mesh):
    return jax.shard_map(
        local,
        mesh=mesh,
        in_specs=(
            P("ctx", "fsdp"),
            P("ctx", None),
            P("ctx", None),
            P("ctx", "fsdp"),
            P("ctx", "fsdp"),
            P("fsdp", None),
            P("fsdp", None),
            P(),
            P("ctx"),
        ),
        out_specs=(P("ctx", "fsdp"), P("fsdp", None), P("fsdp", None)),
        check_vma=False,
    )
```

```python
import functools
import math

import jax
import jax.numpy as jnp
from jax import lax
from jax.experimental import pallas as pl
from jax.experimental.pallas import tpu as pltpu
from jax.sharding import PartitionSpec as P

DH = 128
HPG = 8
KVG = 2
TOK = 128
HALF = TOK // 2
Z = 8
X = 4
C = 2
Y = 4
G = X * C
PAIRS = Z * X * C
HEADS = 4
ROWS = G * TOK
CLIP_RATE = 0.02
EPSILON = 1e-06
NEGATIVE = -1e30
SCALE = 1.0 / math.sqrt(DH)
SCALE2 = SCALE * math.log2(math.e)
MESH = pl.DeviceIdType.MESH
ANY = pl.BlockSpec(memory_space=pl.ANY)
VMEM = pl.BlockSpec(memory_space=pltpu.VMEM)
SMEM = pl.BlockSpec(memory_space=pltpu.SMEM)
LAST = (((1,), (1,)), ((), ()))
FIRST = (((0,), (0,)), ((), ()))
BF16 = jnp.bfloat16
F32 = jnp.float32


class Place:
    def __init__(self):
        me = lax.axis_index("ctx")
        self.me = me
        self.y = lax.axis_index("fsdp")
        self.z = lax.div(me, G)
        self.slot = lax.rem(me, G)
        self.x = lax.div(self.slot, C)
        self.c = lax.rem(self.slot, C)

    def xslot(self, step, flip=False):
        x = lax.rem(self.x + step + X, X)
        return x * C + ((1 - self.c) if flip else self.c)

    def in_plane(self, slot):
        return {"ctx": self.z * G + slot}

    def zslot(self, step):
        return lax.rem(self.z + step + Z, Z)

    def in_column(self, z):
        return {"ctx": z * G + self.slot}

    def yslot(self, step):
        return lax.rem(self.y + step, Y)


class Copies:
    def __init__(self, send, recv):
        self.send, self.recv, self.made = send, recv, []

    def __call__(self, src, dst, device):
        i = len(self.made)
        copy = pltpu.make_async_remote_copy(
            src_ref=src,
            dst_ref=dst,
            send_sem=self.send.at[i],
            recv_sem=self.recv.at[i],
            device_id=device,
            device_id_type=MESH,
        )
        copy.start()
        self.made.append(copy)
        return copy

    def wait_sends(self):
        for copy in self.made:
            copy.wait_send()


def barrier(devices):
    sem = pltpu.get_barrier_semaphore()
    for device in devices:
        pl.semaphore_signal(sem, inc=1, device_id=device, device_id_type=MESH)
    pl.semaphore_wait(sem, len(devices))


def at(slot, rows, offset=0, count=None):
    return pl.ds(pl.multiple_of(slot * rows + offset, 16), rows if count is None else count)


def plane_ring(copies, p, src, where, rows):
    half = rows // 2
    right, left = p.xslot(1), p.xslot(-1)
    far = p.xslot(2)
    partner = p.in_plane(p.xslot(0, True))
    mine = where(p.slot, 0, rows)
    a = copies(src, mine, p.in_plane(right))
    b = copies(src, mine, p.in_plane(left))
    own = copies(src, mine, partner)
    yield
    a.wait_recv()
    first = where(left, 0, half)
    f = copies(first, first, p.in_plane(right))
    block = where(left, 0, rows)
    pa = copies(block, block, partner)
    b.wait_recv()
    second = where(right, half, half)
    g = copies(second, second, p.in_plane(left))
    block = where(right, 0, rows)
    pb = copies(block, block, partner)
    yield
    f.wait_recv()
    g.wait_recv()
    block = where(far, 0, rows)
    pc = copies(block, block, partner)
    yield
    own.wait_recv()
    pa.wait_recv()
    pb.wait_recv()
    pc.wait_recv()


def whole(ref, rows):
    return lambda slot, offset, count: ref.at[at(slot, rows, offset, count)]


def column_ring(copies, p, src, where):
    up, down = p.in_column(p.zslot(1)), p.in_column(p.zslot(-1))
    u = copies(src, where(p.z), up)
    d = copies(src, where(p.z), down)
    for step in range(1, Z // 2 + 1):
        yield
        u.wait_recv()
        if step < Z // 2:
            block = where(p.zslot(-step))
            u = copies(block, block, up)
        if step < Z // 2:
            d.wait_recv()
            if step < Z // 2 - 1:
                block = where(p.zslot(step))
                d = copies(block, block, down)


def run(*rings):
    rings = list(rings)
    while rings:
        rings = [ring for ring in rings if next(ring, True) is None]


def plane_peers(p):
    return [p.in_plane(p.xslot(s, f)) for s in range(X) for f in (False, True) if s or f]


def column_peers(p):
    return [p.in_column(p.zslot(s)) for s in range(1, Z)]


def row_peers(p):
    return [{"fsdp": p.yslot(s)} for s in range(1, Y)]


def sum_squares(ref, chunk=64):
    width = ref.shape[1]

    def step(i, acc):
        block = ref[pl.ds(pl.multiple_of(i * chunk, chunk), chunk), :].astype(F32)
        return acc + jnp.sum((block * block).reshape(chunk // 8, 8, width), axis=0)

    acc = lax.fori_loop(0, ref.shape[0] // chunk, step, jnp.zeros((8, width), F32))
    return jnp.sum(acc, axis=0, keepdims=True)


def gather_kernel(
    q, do, k, v, pos, kw, vw, qg, dog, kg, vg, pg, wsum, tq, tdo, tk, tv, tp, tkw, tvw, send, recv, local
):
    p = Place()
    group = lax.div(p.y * HEADS, HPG)
    cols = pl.ds(pl.multiple_of(group * DH, DH), DH)
    own_k, own_v = k.at[:, cols], v.at[:, cols]
    mine = at(p.slot, TOK)
    moves = [
        (q, tq, qg.at[mine]),
        (do, tdo, dog.at[mine]),
        (own_k, tk, kg.at[at(p.z, TOK)]),
        (own_v, tv, vg.at[at(p.z, TOK)]),
        (pos, tp, pg.at[p.slot]),
    ]
    loads = [pltpu.make_async_copy(s, t, local.at[i]) for i, (s, t, _) in enumerate(moves)]
    for load in loads:
        load.start()
    heavy = [
        pltpu.make_async_copy(s, t, local.at[2 * len(moves) + i])
        for i, (s, t) in enumerate(((kw, tkw), (vw, tvw)))
    ]
    for load in heavy:
        load.start()
    barrier(plane_peers(p) + [p.in_column(p.zslot(1)), p.in_column(p.zslot(-1))])
    copies = Copies(send, recv)
    rings = [
        column_ring(copies, p, own_k, lambda z: kg.at[at(z, TOK)]),
        plane_ring(copies, p, q, whole(qg, TOK), TOK),
        column_ring(copies, p, own_v, lambda z: vg.at[at(z, TOK)]),
        plane_ring(copies, p, do, whole(dog, TOK), TOK),
    ]
    for ring in rings:
        next(ring)
    stores = []
    for i, (_, t, d) in enumerate(moves):
        loads[i].wait()
        store = pltpu.make_async_copy(t, d, local.at[len(moves) + i])
        store.start()
        stores.append(store)
    small = [copies(pos, pg.at[p.slot], peer) for peer in plane_peers(p)]
    for load in heavy:
        load.wait()
    wsum[...] = jnp.broadcast_to(
        jnp.concatenate([sum_squares(tkw), sum_squares(tvw)], axis=1), wsum.shape
    )
    run(*rings)
    for copy in small:
        copy.wait_recv()
    copies.wait_sends()
    for store in stores:
        store.wait()


def tile_bias(owners, pos, bias, j, p, width):
    lane = lax.broadcasted_iota(jnp.int32, (1, TOK), 1)
    low = lane < HALF
    places, floors = [], []
    for s in range(width // TOK):
        slot = j * (width // TOK) + s
        owner = owners[p.z * G + slot]
        place = lane + jnp.where(low, owner * HALF, (2 * PAIRS - 1 - owner) * HALF - HALF)
        places.append(place)
        floors.append(place - pos[slot, 0:1, :])
    place = jnp.concatenate(places, axis=1)
    floor = jnp.concatenate(floors, axis=1)
    row = lax.broadcasted_iota(jnp.int32, (HALF, width), 0)
    for z in range(Z):
        owner = owners[z * G + p.slot]
        for h, stretch in enumerate((owner, 2 * PAIRS - 1 - owner)):
            key = row + stretch * HALF
            seen = (key <= place) & (key >= floor)
            bias[pl.ds(z * TOK + h * HALF, HALF), :] = jnp.where(seen, 0.0, NEGATIVE)


def stats_kernel(owners, pos, q, do, k, v, out, bias):
    p = Place()
    width = q.shape[0]
    tile_bias(owners, pos, bias, pl.program_id(0), p, width)
    for h in range(HEADS):
        cols = pl.ds(h * DH, DH)
        raw = lax.dot_general(k[...], q[:, cols], LAST, preferred_element_type=F32) + bias[...]
        top = jnp.max(raw, axis=0, keepdims=True)
        mass = jnp.exp2((raw - top) * SCALE2)
        total = jnp.sum(mass, axis=0, keepdims=True)
        dp = lax.dot_general(v[...], do[:, cols], LAST, preferred_element_type=F32)
        dsum = jnp.sum(mass * dp, axis=0, keepdims=True)
        out[h : h + 1, :] = top * SCALE2 + jnp.log2(total)
        out[HEADS + h : HEADS + h + 1, :] = dsum / total


def share_kernel(stats, out, send, recv, local):
    p = Place()
    load = pltpu.make_async_copy(stats, out.at[p.slot], local.at[0])
    load.start()
    barrier(plane_peers(p))
    copies = Copies(send, recv)
    made = [copies(stats, out.at[p.slot], peer) for peer in plane_peers(p)]
    for copy in made:
        copy.wait_recv()
    copies.wait_sends()
    load.wait()


def grads_kernel(owners, pos, stats, q, do, k, v, dq, dkv, bias, kt, probs, slopes, acc):
    p = Place()
    j = pl.program_id(0)
    width = q.shape[0]

    @pl.when(j == 0)
    def _():
        kt[...] = k[...].T
        acc[...] = jnp.zeros_like(acc)

    tile_bias(owners, pos, bias, j, p, width)
    for h in range(HEADS):
        cols = pl.ds(h * DH, DH)
        parts = stats[:, h, :]
        top = jnp.max(parts, axis=0, keepdims=True)
        weight = jnp.exp2(parts - top)
        total = jnp.sum(weight, axis=0, keepdims=True)
        lse = top + jnp.log2(total)
        delta = jnp.sum(weight * stats[:, HEADS + h, :], axis=0, keepdims=True) / total
        raw = lax.dot_general(k[...], q[:, cols], LAST, preferred_element_type=F32) + bias[...]
        prob = jnp.exp2(raw * SCALE2 - lse)
        dp = lax.dot_general(v[...], do[:, cols], LAST, preferred_element_type=F32)
        slope = (prob * (dp - delta)).astype(BF16)
        at_h = pl.ds(h * width, width)
        probs[:, at_h] = prob.astype(BF16)
        slopes[:, at_h] = slope
        dqt = jnp.dot(kt[...], slopes[:, at_h], preferred_element_type=F32)
        dq[:, cols] = (dqt * SCALE).T.astype(BF16)
    tall = lambda ref: jnp.concatenate([ref[:, pl.ds(h * DH, DH)] for h in range(HEADS)], axis=0)
    acc[:, :DH] += jnp.dot(slopes[...], tall(q), preferred_element_type=F32)
    acc[:, DH:] += jnp.dot(probs[...], tall(do), preferred_element_type=F32)

    @pl.when(j == pl.num_programs(0) - 1)
    def _():
        dkv[:, :DH] = (acc[:, :DH] * SCALE).astype(BF16)
        dkv[:, DH:] = acc[:, DH:].astype(BF16)


def reduce_kernel(
    dq, dkv, hid, dq_slots, grads, hg, th, dqa, pq, cq, gz, ysend, gy, both, send, recv, local
):
    p = Place()
    wide = hid.shape[1] // G
    mine = at(p.slot, TOK)

    def strip(slot):
        return hid.at[:, pl.ds(pl.multiple_of(slot * wide, 128), wide)]

    own_h = pltpu.make_async_copy(strip(p.slot), th, local.at[0])
    own_h.start()
    own_g = pltpu.make_async_copy(dkv.at[at(p.z, TOK)], gz.at[p.z], local.at[1])
    own_g.start()
    kept = [
        pltpu.make_async_copy(dq.at[at(x * C + p.c, TOK)], dqa.at[x], local.at[5 + x])
        for x in range(X)
    ]
    for load in kept:
        load.start()
    barrier(plane_peers(p) + column_peers(p) + row_peers(p))
    copies = Copies(send, recv)
    zs = [
        copies(dkv.at[at(p.zslot(s), TOK)], gz.at[p.z], p.in_column(p.zslot(s)))
        for s in (4, 3, 5, 2, 6, 1, 7)
    ]
    partner = p.in_plane(p.xslot(0, True))
    given = [copies(dq.at[at(x * C + 1 - p.c, TOK)], pq.at[x], partner) for x in range(X)]
    hs = []
    for s, f in ((2, False), (2, True), (1, False), (3, False), (1, True), (3, True), (0, True)):
        to = p.xslot(s, f)
        hs.append(copies(strip(to), hg.at[mine], p.in_plane(to)))
    own_h.wait()
    put_h = pltpu.make_async_copy(th, hg.at[mine], local.at[2])
    put_h.start()
    for x in range(X):
        kept[x].wait()
        given[x].wait_recv()
        cq[x] = (dqa[x].astype(F32) + pq[x].astype(F32)).astype(BF16)
    qs = []
    for s in (2, 1, 3):
        to = lax.rem(p.x + s, X)
        qs.append(copies(cq.at[to], dq_slots.at[p.x], p.in_plane(to * C + p.c)))
    put_q = pltpu.make_async_copy(cq.at[p.x], dq_slots.at[p.x], local.at[3])
    put_q.start()
    own_g.wait()
    for copy in zs:
        copy.wait_recv()
    total = gz[0].astype(F32)
    for z in range(1, Z):
        total = total + gz[z].astype(F32)
    ysend[...] = total.astype(BF16)
    gy[p.y] = total.astype(BF16)
    ys = [copies(ysend, gy.at[p.y], peer) for peer in row_peers(p)]
    for copy in ys:
        copy.wait_recv()
    members = Y // KVG
    for g in range(KVG):
        part = gy[g * members].astype(F32)
        for i in range(1, members):
            part = part + gy[g * members + i].astype(F32)
        both[:, g * DH : (g + 1) * DH] = part[:, :DH].astype(BF16)
        both[:, (KVG + g) * DH : (KVG + g + 1) * DH] = part[:, DH:].astype(BF16)
    put_g = pltpu.make_async_copy(both, grads.at[mine], local.at[4])
    put_g.start()
    run(plane_ring(copies, p, both, whole(grads, TOK), TOK))
    for copy in qs + hs:
        copy.wait_recv()
    copies.wait_sends()
    for put in (put_h, put_q, put_g):
        put.wait()


def finish_kernel(part, weights, raw, sums, rz, ysum, send, recv, local):
    p = Place()
    rows = part.shape[0]
    piece = rows // Z
    width = raw.shape[1]
    own = pltpu.make_async_copy(part.at[at(p.z, piece)], rz.at[p.z], local.at[0])
    own.start()
    barrier(plane_peers(p) + column_peers(p) + row_peers(p))
    copies = Copies(send, recv)
    zs = [
        copies(part.at[at(p.zslot(s), piece)], rz.at[p.z], p.in_column(p.zslot(s)))
        for s in (4, 3, 5, 2, 6, 1, 7)
    ]
    own.wait()
    for copy in zs:
        copy.wait_recv()
    total = rz[0].astype(F32)
    for z in range(1, Z):
        total = total + rz[z].astype(F32)

    def where(slot, z, offset=0, count=piece):
        return pl.ds(pl.multiple_of(slot * rows + z * piece + offset, 16), count)

    raw[where(p.slot, p.z), :] = total.astype(BF16)
    column = column_ring(copies, p, raw.at[where(p.slot, p.z)], lambda z: raw.at[where(p.slot, z)])
    next(column)

    def ring(z):
        made = plane_ring(
            copies,
            p,
            raw.at[where(p.slot, z)],
            lambda slot, offset, count: raw.at[where(slot, z, offset, count)],
            piece,
        )
        next(made)
        return made

    waves = [[ring(p.z)]]
    for s in range(1, Z // 2 + 1):
        next(column, None)
        waves.append([ring(p.zslot(d)) for d in ((-s, s) if s < Z // 2 else (-s,))])
        for wave in waves[max(0, s - 2) : s][::-1]:
            for made in wave:
                next(made)
    square = sum_squares(raw.at[at(p.slot, rows)])
    row = lax.broadcasted_iota(jnp.int32, (8, width), 0)
    ysum[p.y] = jnp.where(row == 0, square, weights[...])
    ys = [copies(ysum.at[p.y], ysum.at[p.y], peer) for peer in row_peers(p)]
    for wave in waves[Z // 2 - 1 :]:
        for made in wave:
            next(made)
    for copy in ys:
        copy.wait_recv()
    sums[p.slot] = ysum[0] + ysum[1] + ysum[2] + ysum[3]
    shares = [copies(sums.at[p.slot], sums.at[p.slot], peer) for peer in plane_peers(p)]
    run(*[made for wave in waves for made in wave])
    for copy in shares:
        copy.wait_recv()
    copies.wait_sends()


def remote(ident, kernel, **kw):
    return pl.pallas_call(
        kernel,
        compiler_params=pltpu.CompilerParams(
            collective_id=ident, has_side_effects=True, vmem_limit_bytes=40 * 1024 * 1024
        ),
        **kw,
    )


def shape(dims, kind=BF16):
    return jax.ShapeDtypeStruct(dims, kind)


def dma(n):
    return pltpu.SemaphoreType.DMA((n,))


def local(
    queries, keys, values, out_grad, hidden, key_weight, value_weight, stretch_owner, positions
):
    width = queries.shape[1]
    model = hidden.shape[1]
    piece = model // G
    columns = KVG * DH
    pos = jnp.broadcast_to(positions[None, :], (8, TOK))
    qg, dog, kg, vg, pg, weights = remote(
        0,
        gather_kernel,
        out_shape=(
            shape((ROWS, width)),
            shape((ROWS, width)),
            shape((Z * TOK, DH)),
            shape((Z * TOK, DH)),
            shape((G, 8, TOK), jnp.int32),
            shape((8, 2 * columns), F32),
        ),
        in_specs=[ANY] * 7,
        out_specs=(ANY,) * 5 + (VMEM,),
        scratch_shapes=[
            pltpu.VMEM((TOK, width), BF16),
            pltpu.VMEM((TOK, width), BF16),
            pltpu.VMEM((TOK, DH), BF16),
            pltpu.VMEM((TOK, DH), BF16),
            pltpu.VMEM((8, TOK), jnp.int32),
            pltpu.VMEM((model, columns), BF16),
            pltpu.VMEM((model, columns), BF16),
            dma(48),
            dma(48),
            dma(12),
        ],
    )(queries, out_grad, keys, values, pos, key_weight, value_weight)
    tile = 256
    q_spec = pl.BlockSpec((tile, width), lambda j: (j, 0))
    k_spec = pl.BlockSpec((Z * TOK, DH), lambda j: (0, 0))
    pos_spec = pl.BlockSpec((G, 8, TOK), lambda j: (0, 0, 0))
    params = pltpu.CompilerParams(
        dimension_semantics=("arbitrary",), vmem_limit_bytes=48 * 1024 * 1024
    )
    stats = pl.pallas_call(
        stats_kernel,
        grid=(ROWS // tile,),
        out_shape=shape((2 * HEADS, ROWS), F32),
        in_specs=[SMEM, pos_spec, q_spec, q_spec, k_spec, k_spec],
        out_specs=pl.BlockSpec((2 * HEADS, tile), lambda j: (0, j)),
        scratch_shapes=[pltpu.VMEM((Z * TOK, tile), F32)],
        compiler_params=params,
    )(stretch_owner, pg, qg, dog, kg, vg)
    shared = remote(
        1,
        share_kernel,
        out_shape=shape((G, 2 * HEADS, ROWS), F32),
        in_specs=[VMEM],
        out_specs=VMEM,
        scratch_shapes=[dma(8), dma(8), dma(1)],
    )(stats)
    dq, dkv = pl.pallas_call(
        grads_kernel,
        grid=(ROWS // tile,),
        out_shape=(shape((ROWS, width)), shape((Z * TOK, 2 * DH))),
        in_specs=[
            SMEM,
            pos_spec,
            pl.BlockSpec((G, 2 * HEADS, tile), lambda j: (0, 0, j)),
            q_spec,
            q_spec,
            k_spec,
            k_spec,
        ],
        out_specs=(q_spec, pl.BlockSpec((Z * TOK, 2 * DH), lambda j: (0, 0))),
        scratch_shapes=[
            pltpu.VMEM((Z * TOK, tile), F32),
            pltpu.VMEM((DH, Z * TOK), BF16),
            pltpu.VMEM((Z * TOK, HEADS * tile), BF16),
            pltpu.VMEM((Z * TOK, HEADS * tile), BF16),
            pltpu.VMEM((Z * TOK, 2 * DH), F32),
        ],
        compiler_params=params,
    )(stretch_owner, pg, shared, qg, dog, kg, vg)
    dq_slots, grads, hg = remote(
        2,
        reduce_kernel,
        out_shape=(shape((X, TOK, width)), shape((ROWS, 2 * columns)), shape((ROWS, piece))),
        in_specs=[ANY, ANY, ANY],
        out_specs=(ANY, ANY, ANY),
        scratch_shapes=[
            pltpu.VMEM((TOK, piece), BF16),
            pltpu.VMEM((X, TOK, width), BF16),
            pltpu.VMEM((X, TOK, width), BF16),
            pltpu.VMEM((X, TOK, width), BF16),
            pltpu.VMEM((Z, TOK, 2 * DH), BF16),
            pltpu.VMEM((TOK, 2 * DH), BF16),
            pltpu.VMEM((Y, TOK, 2 * DH), BF16),
            pltpu.VMEM((TOK, 2 * columns), BF16),
            dma(40),
            dma(40),
            dma(9),
        ],
    )(dq, dkv, hidden)
    query_grad = jnp.sum(dq_slots.astype(F32), axis=0).astype(BF16)
    part = lax.dot_general(hg, grads, FIRST, preferred_element_type=F32).astype(BF16)
    raw, sums = remote(
        3,
        finish_kernel,
        out_shape=(shape((model, 2 * columns)), shape((G, 8, 2 * columns), F32)),
        in_specs=[ANY, VMEM],
        out_specs=(VMEM, VMEM),
        scratch_shapes=[
            pltpu.VMEM((Z, piece // Z, 2 * columns), BF16),
            pltpu.VMEM((Y, 8, 2 * columns), F32),
            dma(112),
            dma(112),
            dma(1),
        ],
    )(part, weights)
    grad_norm = jnp.sqrt(jnp.sum(sums[:, 0], axis=0) + EPSILON)
    weight_norm = jnp.sqrt(sums[0, 1] + EPSILON)
    tokens = TOK * PAIRS
    factor = jnp.minimum(1.0, CLIP_RATE * tokens * weight_norm / grad_norm)
    key_out = raw[:, :columns].astype(F32) * factor[None, :columns]
    value_out = raw[:, columns:].astype(F32) * factor[None, columns:]
    return (query_grad, key_out, value_out)


def solution(mesh):
    return jax.shard_map(
        local,
        mesh=mesh,
        in_specs=(
            P("ctx", "fsdp"),
            P("ctx", None),
            P("ctx", None),
            P("ctx", "fsdp"),
            P("ctx", "fsdp"),
            P("fsdp", None),
            P("fsdp", None),
            P(),
            P("ctx"),
        ),
        out_specs=(P("ctx", "fsdp"), P("fsdp", None), P("fsdp", None)),
        check_vma=False,
    )
```

```python
import functools
import math

import jax
import jax.numpy as jnp
from jax import lax
from jax.experimental import pallas as pl
from jax.experimental.pallas import tpu as pltpu
from jax.sharding import PartitionSpec as P

DH = 128
HPG = 8
KVG = 2
TOK = 128
HALF = TOK // 2
Z = 8
X = 4
C = 2
Y = 4
G = X * C
PAIRS = Z * X * C
HEADS = 4
ROWS = G * TOK
CLIP_RATE = 0.02
EPSILON = 1e-06
NEGATIVE = -1e30
SCALE = 1.0 / math.sqrt(DH)
SCALE2 = SCALE * math.log2(math.e)
MESH = pl.DeviceIdType.MESH
ANY = pl.BlockSpec(memory_space=pl.ANY)
VMEM = pl.BlockSpec(memory_space=pltpu.VMEM)
HBM = pl.BlockSpec(memory_space=pltpu.HBM)
SMEM = pl.BlockSpec(memory_space=pltpu.SMEM)
LAST = (((1,), (1,)), ((), ()))
FIRST = (((0,), (0,)), ((), ()))
BF16 = jnp.bfloat16
F32 = jnp.float32


class Place:
    def __init__(self):
        me = lax.axis_index("ctx")
        self.me = me
        self.y = lax.axis_index("fsdp")
        self.z = lax.div(me, G)
        self.slot = lax.rem(me, G)
        self.x = lax.div(self.slot, C)
        self.c = lax.rem(self.slot, C)

    def xslot(self, step, flip=False):
        x = lax.rem(self.x + step + X, X)
        return x * C + ((1 - self.c) if flip else self.c)

    def in_plane(self, slot):
        return {"ctx": self.z * G + slot}

    def zslot(self, step):
        return lax.rem(self.z + step + Z, Z)

    def in_column(self, z):
        return {"ctx": z * G + self.slot}

    def yslot(self, step):
        return lax.rem(self.y + step, Y)


class Copies:
    def __init__(self, send, recv):
        self.send, self.recv, self.made = send, recv, []

    def __call__(self, src, dst, device):
        i = len(self.made)
        copy = pltpu.make_async_remote_copy(
            src_ref=src,
            dst_ref=dst,
            send_sem=self.send.at[i],
            recv_sem=self.recv.at[i],
            device_id=device,
            device_id_type=MESH,
        )
        copy.start()
        self.made.append(copy)
        return copy

    def wait_sends(self):
        for copy in self.made:
            copy.wait_send()


def barrier(devices):
    sem = pltpu.get_barrier_semaphore()
    for device in devices:
        pl.semaphore_signal(sem, inc=1, device_id=device, device_id_type=MESH)
    pl.semaphore_wait(sem, len(devices))


def at(slot, rows, offset=0, count=None):
    return pl.ds(pl.multiple_of(slot * rows + offset, 16), rows if count is None else count)


def plane_ring(copies, p, src, where, rows):
    half = rows // 2
    right, left = p.xslot(1), p.xslot(-1)
    far = p.xslot(2)
    partner = p.in_plane(p.xslot(0, True))
    mine = where(p.slot, 0, rows)
    a = copies(src, mine, p.in_plane(right))
    b = copies(src, mine, p.in_plane(left))
    own = copies(src, mine, partner)
    yield
    a.wait_recv()
    first = where(left, 0, half)
    f = copies(first, first, p.in_plane(right))
    block = where(left, 0, rows)
    pa = copies(block, block, partner)
    b.wait_recv()
    second = where(right, half, half)
    g = copies(second, second, p.in_plane(left))
    block = where(right, 0, rows)
    pb = copies(block, block, partner)
    yield
    f.wait_recv()
    g.wait_recv()
    block = where(far, 0, rows)
    pc = copies(block, block, partner)
    yield
    own.wait_recv()
    pa.wait_recv()
    pb.wait_recv()
    pc.wait_recv()


def whole(ref, rows):
    return lambda slot, offset, count: ref.at[at(slot, rows, offset, count)]


def column_ring(copies, p, src, where):
    up, down = p.in_column(p.zslot(1)), p.in_column(p.zslot(-1))
    u = copies(src, where(p.z), up)
    d = copies(src, where(p.z), down)
    for step in range(1, Z // 2 + 1):
        yield
        u.wait_recv()
        if step < Z // 2:
            block = where(p.zslot(-step))
            u = copies(block, block, up)
        if step < Z // 2:
            d.wait_recv()
            if step < Z // 2 - 1:
                block = where(p.zslot(step))
                d = copies(block, block, down)


def run(*rings):
    rings = list(rings)
    while rings:
        rings = [ring for ring in rings if next(ring, True) is None]


def plane_peers(p):
    return [p.in_plane(p.xslot(s, f)) for s in range(X) for f in (False, True) if s or f]


def column_peers(p):
    return [p.in_column(p.zslot(s)) for s in range(1, Z)]


def row_peers(p):
    return [{"fsdp": p.yslot(s)} for s in range(1, Y)]


def sum_squares(ref, chunk=64):
    width = ref.shape[1]

    def step(i, acc):
        block = ref[pl.ds(pl.multiple_of(i * chunk, chunk), chunk), :].astype(F32)
        return acc + jnp.sum((block * block).reshape(chunk // 8, 8, width), axis=0)

    acc = lax.fori_loop(0, ref.shape[0] // chunk, step, jnp.zeros((8, width), F32))
    return jnp.sum(acc, axis=0, keepdims=True)


def gather_kernel(q, do, k, v, pos, qg, dog, kg, vg, pg, tq, tdo, tk, tv, send, recv, local):
    p = Place()
    group = lax.div(p.y * HEADS, HPG)
    cols = pl.ds(pl.multiple_of(group * DH, DH), DH)
    own_k, own_v = k.at[:, cols], v.at[:, cols]
    mine = at(p.slot, TOK)
    moves = [
        (q, tq, qg.at[mine]),
        (do, tdo, dog.at[mine]),
        (own_k, tk, kg.at[at(p.z, TOK)]),
        (own_v, tv, vg.at[at(p.z, TOK)]),
    ]
    loads = [pltpu.make_async_copy(s, t, local.at[i]) for i, (s, t, _) in enumerate(moves)]
    for load in loads:
        load.start()
    pg[p.slot] = jnp.broadcast_to(pos[...], (8, TOK))
    barrier(plane_peers(p) + [p.in_column(p.zslot(1)), p.in_column(p.zslot(-1))])
    copies = Copies(send, recv)
    kr = column_ring(copies, p, own_k, lambda z: kg.at[at(z, TOK)])
    vr = column_ring(copies, p, own_v, lambda z: vg.at[at(z, TOK)])
    qr = plane_ring(copies, p, q, whole(qg, TOK), TOK)
    dr = plane_ring(copies, p, do, whole(dog, TOK), TOK)
    for ring in (kr, vr, qr, dr):
        next(ring)
    stores = []
    for i, (_, t, d) in enumerate(moves):
        loads[i].wait()
        store = pltpu.make_async_copy(t, d, local.at[len(moves) + i])
        store.start()
        stores.append(store)
    small = [copies(pg.at[p.slot], pg.at[p.slot], peer) for peer in plane_peers(p)]
    for ring in (kr, vr, kr, vr, qr, kr, vr, dr, kr, vr, qr, dr):
        next(ring, None)
    run(qr, dr)
    for copy in small:
        copy.wait_recv()
    copies.wait_sends()
    for store in stores:
        store.wait()


def tile_bias(owners, pos, bias, j, p, width):
    lane = lax.broadcasted_iota(jnp.int32, (1, TOK), 1)
    low = lane < HALF
    places, floors = [], []
    for s in range(width // TOK):
        slot = j * (width // TOK) + s
        owner = owners[p.z * G + slot]
        place = lane + jnp.where(low, owner * HALF, (2 * PAIRS - 1 - owner) * HALF - HALF)
        places.append(place)
        floors.append(place - pos[slot, 0:1, :])
    place = jnp.concatenate(places, axis=1)
    floor = jnp.concatenate(floors, axis=1)
    row = lax.broadcasted_iota(jnp.int32, (HALF, width), 0)
    for z in range(Z):
        owner = owners[z * G + p.slot]
        for h, stretch in enumerate((owner, 2 * PAIRS - 1 - owner)):
            key = row + stretch * HALF
            seen = (key <= place) & (key >= floor)
            bias[pl.ds(z * TOK + h * HALF, HALF), :] = jnp.where(seen, 0.0, NEGATIVE)


def stats_kernel(owners, pos, q, do, k, v, out, bias):
    p = Place()
    width = q.shape[0]
    tile_bias(owners, pos, bias, pl.program_id(0), p, width)
    for h in range(HEADS):
        cols = pl.ds(h * DH, DH)
        raw = lax.dot_general(k[...], q[:, cols], LAST, preferred_element_type=F32) + bias[...]
        top = jnp.max(raw, axis=0, keepdims=True)
        mass = jnp.exp2((raw - top) * SCALE2)
        total = jnp.sum(mass, axis=0, keepdims=True)
        dp = lax.dot_general(v[...], do[:, cols], LAST, preferred_element_type=F32)
        dsum = jnp.sum(mass * dp, axis=0, keepdims=True)
        out[h : h + 1, :] = top * SCALE2 + jnp.log2(total)
        out[HEADS + h : HEADS + h + 1, :] = dsum / total


def share_kernel(stats, out, send, recv, local):
    p = Place()
    load = pltpu.make_async_copy(stats, out.at[p.slot], local.at[0])
    load.start()
    barrier(plane_peers(p))
    copies = Copies(send, recv)
    made = [copies(stats, out.at[p.slot], peer) for peer in plane_peers(p)]
    for copy in made:
        copy.wait_recv()
    copies.wait_sends()
    load.wait()


def grads_kernel(owners, pos, stats, q, do, k, v, dq, dk, dv, bias, kt, probs, slopes, acc):
    p = Place()
    j = pl.program_id(0)
    width = q.shape[0]

    @pl.when(j == 0)
    def _():
        kt[...] = k[...].T
        acc[...] = jnp.zeros_like(acc)

    tile_bias(owners, pos, bias, j, p, width)
    for h in range(HEADS):
        cols = pl.ds(h * DH, DH)
        parts = stats[:, h, :]
        top = jnp.max(parts, axis=0, keepdims=True)
        weight = jnp.exp2(parts - top)
        total = jnp.sum(weight, axis=0, keepdims=True)
        lse = top + jnp.log2(total)
        delta = jnp.sum(weight * stats[:, HEADS + h, :], axis=0, keepdims=True) / total
        raw = lax.dot_general(k[...], q[:, cols], LAST, preferred_element_type=F32) + bias[...]
        prob = jnp.exp2(raw * SCALE2 - lse)
        dp = lax.dot_general(v[...], do[:, cols], LAST, preferred_element_type=F32)
        slope = (prob * (dp - delta)).astype(BF16)
        at_h = pl.ds(h * width, width)
        probs[:, at_h] = prob.astype(BF16)
        slopes[:, at_h] = slope
        dqt = jnp.dot(kt[...], slopes[:, at_h], preferred_element_type=F32)
        dq[:, cols] = (dqt * SCALE).T.astype(BF16)
    tall = lambda ref: jnp.concatenate([ref[:, pl.ds(h * DH, DH)] for h in range(HEADS)], axis=0)
    acc[:, :DH] += jnp.dot(slopes[...], tall(q), preferred_element_type=F32)
    acc[:, DH:] += jnp.dot(probs[...], tall(do), preferred_element_type=F32)

    @pl.when(j == pl.num_programs(0) - 1)
    def _():
        dk[...] = (acc[:, :DH] * SCALE).astype(BF16)
        dv[...] = acc[:, DH:].astype(BF16)


FARTHEST = (4, 3, 5, 2, 6, 1, 7)


def rounded_sum(ref, i, count):
    total = ref[i, 0].astype(F32)
    for n in range(1, count):
        total = total + ref[i, n].astype(F32)
    return total.astype(BF16)


def tail_kernel(
    dq, dk, dv, hid, kw, vw, dq_slots, raw_k, raw_v, sums,
    hg, hgt, dqa, pq, cq, gz, gy, grads, part, rz, ysum, wsum, tw, send, recv, local
):
    p = Place()
    wide = hid.shape[1] // G
    piece = wide // Z
    mine = at(p.slot, TOK)
    members = Y // KVG

    def strip(slot):
        return hid.at[:, pl.ds(pl.multiple_of(slot * wide, 128), wide)]

    kept = [
        pltpu.make_async_copy(dq.at[at(x * C + p.c, TOK)], dqa.at[x], local.at[x])
        for x in range(X)
    ]
    own_g = [
        pltpu.make_async_copy(src.at[at(p.z, TOK)], gz.at[i, p.z], local.at[X + i])
        for i, src in enumerate((dk, dv))
    ]
    own_h = pltpu.make_async_copy(strip(p.slot), hg.at[mine], local.at[X + 2])
    loads = [pltpu.make_async_copy(w, tw.at[i], local.at[X + 3 + i]) for i, w in enumerate((kw, vw))]
    for load in kept + own_g + [own_h] + loads:
        load.start()
    barrier(plane_peers(p) + column_peers(p) + row_peers(p))
    copies = Copies(send, recv)

    def stream(i, src, raw):
        made = [
            copies(src.at[at(p.zslot(s), TOK)], gz.at[i, p.z], p.in_column(p.zslot(s)))
            for s in FARTHEST
        ]
        yield
        own_g[i].wait()
        for copy in made:
            copy.wait_recv()
        gy[i, p.y] = rounded_sum(gz, i, Z)
        made = [copies(gy.at[i, p.y], gy.at[i, p.y], peer) for peer in row_peers(p)]
        yield
        for copy in made:
            copy.wait_recv()
        for g in range(KVG):
            total = gy[i, g * members].astype(F32)
            for n in range(1, members):
                total = total + gy[i, g * members + n].astype(F32)
            grads[i, mine, g * DH : (g + 1) * DH] = total.astype(BF16)
        ring = plane_ring(copies, p, grads.at[i, mine], whole(grads.at[i], TOK), TOK)
        for _ in ring:
            yield
        product = jnp.dot(hgt[...], grads[i], preferred_element_type=F32)
        part[i] = product.astype(BF16)
        rz[i, p.z] = part[i, at(p.z, piece), :]
        made = [
            copies(part.at[i, at(p.zslot(s), piece)], rz.at[i, p.z], p.in_column(p.zslot(s)))
            for s in FARTHEST
        ]
        yield
        for copy in made:
            copy.wait_recv()
        own = pl.ds(pl.multiple_of(p.slot * wide + p.z * piece, 16), piece)
        raw[own, :] = rounded_sum(rz, i, Z)
        made = [
            copies(raw.at[own], raw.at[own], p.in_column(p.zslot(s))) for s in FARTHEST
        ]
        yield
        for copy in made:
            copy.wait_recv()
        ring = plane_ring(copies, p, raw.at[at(p.slot, wide)], whole(raw, wide), wide)
        next(ring)
        square = sum_squares(raw.at[at(p.slot, wide)])
        row = lax.broadcasted_iota(jnp.int32, (8, square.shape[1]), 0)
        ysum[i, p.y] = jnp.where(row == 0, square, wsum[i])
        made = [copies(ysum.at[i, p.y], ysum.at[i, p.y], peer) for peer in row_peers(p)]
        yield
        next(ring)
        for copy in made:
            copy.wait_recv()
        total = ysum[i, 0]
        for n in range(1, Y):
            total = total + ysum[i, n]
        sums[i, p.slot] = total
        made = [copies(sums.at[i, p.slot], sums.at[i, p.slot], peer) for peer in plane_peers(p)]
        yield
        next(ring)
        yield
        for _ in ring:
            pass
        for copy in made:
            copy.wait_recv()

    streams = [stream(0, dk, raw_k), stream(1, dv, raw_v)]
    for one in streams:
        next(one)
    partner = p.in_plane(p.xslot(0, True))
    given = [copies(dq.at[at(x * C + 1 - p.c, TOK)], pq.at[x], partner) for x in range(X)]
    hs = []
    for s, f in ((2, False), (2, True), (1, False), (3, False), (1, True), (3, True), (0, True)):
        to = p.xslot(s, f)
        hs.append(copies(strip(to), hg.at[mine], p.in_plane(to)))
    for x in range(X):
        kept[x].wait()
        given[x].wait_recv()
        cq[x] = (dqa[x].astype(F32) + pq[x].astype(F32)).astype(BF16)
    qs = []
    for s in (2, 1, 3):
        to = lax.rem(p.x + s, X)
        qs.append(copies(cq.at[to], dq_slots.at[p.x], p.in_plane(to * C + p.c)))
    put_q = pltpu.make_async_copy(cq.at[p.x], dq_slots.at[p.x], local.at[X + 5])
    put_q.start()
    for i, load in enumerate(loads):
        load.wait()
        wsum[i] = jnp.broadcast_to(sum_squares(tw.at[i]), wsum.shape[1:])
    for one in streams:
        next(one)
    own_h.wait()
    for copy in hs:
        copy.wait_recv()
    hgt[...] = hg[...].T
    run(*streams)
    for copy in qs:
        copy.wait_recv()
    copies.wait_sends()
    put_q.wait()


def remote(ident, kernel, **kw):
    return pl.pallas_call(
        kernel,
        compiler_params=pltpu.CompilerParams(
            collective_id=ident, has_side_effects=True, vmem_limit_bytes=40 * 1024 * 1024
        ),
        **kw,
    )


def shape(dims, kind=BF16):
    return jax.ShapeDtypeStruct(dims, kind)


def dma(n):
    return pltpu.SemaphoreType.DMA((n,))


def local(
    queries, keys, values, out_grad, hidden, key_weight, value_weight, stretch_owner, positions
):
    width = queries.shape[1]
    model = hidden.shape[1]
    piece = model // G
    columns = KVG * DH
    qg, dog, kg, vg, pg = remote(
        0,
        gather_kernel,
        out_shape=(
            shape((ROWS, width)),
            shape((ROWS, width)),
            shape((Z * TOK, DH)),
            shape((Z * TOK, DH)),
            shape((G, 8, TOK), jnp.int32),
        ),
        in_specs=[HBM] * 4 + [VMEM],
        out_specs=(ANY,) * 4 + (VMEM,),
        scratch_shapes=[
            pltpu.VMEM((TOK, width), BF16),
            pltpu.VMEM((TOK, width), BF16),
            pltpu.VMEM((TOK, DH), BF16),
            pltpu.VMEM((TOK, DH), BF16),
            dma(48),
            dma(48),
            dma(8),
        ],
    )(queries, out_grad, keys, values, positions.reshape(1, TOK))
    tile = 256
    q_spec = pl.BlockSpec((tile, width), lambda j: (j, 0))
    k_spec = pl.BlockSpec((Z * TOK, DH), lambda j: (0, 0))
    pos_spec = pl.BlockSpec((G, 8, TOK), lambda j: (0, 0, 0))
    params = pltpu.CompilerParams(
        dimension_semantics=("arbitrary",), vmem_limit_bytes=48 * 1024 * 1024
    )
    stats = pl.pallas_call(
        stats_kernel,
        grid=(ROWS // tile,),
        out_shape=shape((2 * HEADS, ROWS), F32),
        in_specs=[SMEM, pos_spec, q_spec, q_spec, k_spec, k_spec],
        out_specs=pl.BlockSpec((2 * HEADS, tile), lambda j: (0, j)),
        scratch_shapes=[pltpu.VMEM((Z * TOK, tile), F32)],
        compiler_params=params,
    )(stretch_owner, pg, qg, dog, kg, vg)
    shared = remote(
        1,
        share_kernel,
        out_shape=shape((G, 2 * HEADS, ROWS), F32),
        in_specs=[VMEM],
        out_specs=VMEM,
        scratch_shapes=[dma(8), dma(8), dma(1)],
    )(stats)
    dq, dk, dv = pl.pallas_call(
        grads_kernel,
        grid=(ROWS // tile,),
        out_shape=(shape((ROWS, width)), shape((Z * TOK, DH)), shape((Z * TOK, DH))),
        in_specs=[
            SMEM,
            pos_spec,
            pl.BlockSpec((G, 2 * HEADS, tile), lambda j: (0, 0, j)),
            q_spec,
            q_spec,
            k_spec,
            k_spec,
        ],
        out_specs=(q_spec, k_spec, k_spec),
        scratch_shapes=[
            pltpu.VMEM((Z * TOK, tile), F32),
            pltpu.VMEM((DH, Z * TOK), BF16),
            pltpu.VMEM((Z * TOK, HEADS * tile), BF16),
            pltpu.VMEM((Z * TOK, HEADS * tile), BF16),
            pltpu.VMEM((Z * TOK, 2 * DH), F32),
        ],
        compiler_params=params,
    )(stretch_owner, pg, shared, qg, dog, kg, vg)
    dq_slots, raw_k, raw_v, sums = remote(
        2,
        tail_kernel,
        out_shape=(
            shape((X, TOK, width)),
            shape((model, columns)),
            shape((model, columns)),
            shape((2, G, 8, columns), F32),
        ),
        in_specs=[ANY] * 3 + [HBM] * 3,
        out_specs=(ANY, VMEM, VMEM, VMEM),
        scratch_shapes=[
            pltpu.VMEM((ROWS, piece), BF16),
            pltpu.VMEM((piece, ROWS), BF16),
            pltpu.VMEM((X, TOK, width), BF16),
            pltpu.VMEM((X, TOK, width), BF16),
            pltpu.VMEM((X, TOK, width), BF16),
            pltpu.VMEM((2, Z, TOK, DH), BF16),
            pltpu.VMEM((2, Y, TOK, DH), BF16),
            pltpu.VMEM((2, ROWS, columns), BF16),
            pltpu.VMEM((2, piece, columns), BF16),
            pltpu.VMEM((2, Z, piece // Z, columns), BF16),
            pltpu.VMEM((2, Y, 8, columns), F32),
            pltpu.VMEM((2, 8, columns), F32),
            pltpu.VMEM((2, model, columns), BF16),
            dma(128),
            dma(128),
            dma(10),
        ],
    )(dq, dk, dv, hidden, key_weight, value_weight)
    query_grad = jnp.sum(dq_slots.astype(F32), axis=0).astype(BF16)
    tokens = TOK * PAIRS

    def clipped(i, raw):
        grad_norm = jnp.sqrt(jnp.sum(sums[i, :, 0], axis=0) + EPSILON)
        weight_norm = jnp.sqrt(sums[i, 0, 1] + EPSILON)
        factor = jnp.minimum(1.0, CLIP_RATE * tokens * weight_norm / grad_norm)
        return raw.astype(F32) * factor[None, :]

    return (query_grad, clipped(0, raw_k), clipped(1, raw_v))


def solution(mesh):
    return jax.shard_map(
        local,
        mesh=mesh,
        in_specs=(
            P("ctx", "fsdp"),
            P("ctx", None),
            P("ctx", None),
            P("ctx", "fsdp"),
            P("ctx", "fsdp"),
            P("fsdp", None),
            P("fsdp", None),
            P(),
            P("ctx"),
        ),
        out_specs=(P("ctx", "fsdp"), P("fsdp", None), P("fsdp", None)),
        check_vma=False,
    )
```

```python
import functools
import math

import jax
import jax.numpy as jnp
from jax import lax
from jax.experimental import pallas as pl
from jax.experimental.pallas import tpu as pltpu
from jax.sharding import PartitionSpec as P

DH = 128
HPG = 8
KVG = 2
TOK = 128
HALF = TOK // 2
Z = 8
X = 4
C = 2
Y = 4
G = X * C
PAIRS = Z * X * C
HEADS = 4
ROWS = G * TOK
CLIP_RATE = 0.02
TILE = 256
VMEM_BYTES = 62 * 1024 * 1024
EPSILON = 1e-06
NEGATIVE = -1e30
SCALE = 1.0 / math.sqrt(DH)
SCALE2 = SCALE * math.log2(math.e)
MESH = pl.DeviceIdType.MESH
ANY = pl.BlockSpec(memory_space=pl.ANY)
VMEM = pl.BlockSpec(memory_space=pltpu.VMEM)
HBM = pl.BlockSpec(memory_space=pltpu.HBM)
SMEM = pl.BlockSpec(memory_space=pltpu.SMEM)
LAST = (((1,), (1,)), ((), ()))
FIRST = (((0,), (0,)), ((), ()))
BF16 = jnp.bfloat16
F32 = jnp.float32


class Place:
    def __init__(self):
        me = lax.axis_index("ctx")
        self.me = me
        self.y = lax.axis_index("fsdp")
        self.z = lax.div(me, G)
        self.slot = lax.rem(me, G)
        self.x = lax.div(self.slot, C)
        self.c = lax.rem(self.slot, C)

    def xslot(self, step, flip=False):
        x = lax.rem(self.x + step + X, X)
        return x * C + ((1 - self.c) if flip else self.c)

    def in_plane(self, slot):
        return {"ctx": self.z * G + slot}

    def zslot(self, step):
        return lax.rem(self.z + step + Z, Z)

    def in_column(self, z):
        return {"ctx": z * G + self.slot}

    def yslot(self, step):
        return lax.rem(self.y + step, Y)


class Copies:
    def __init__(self, send, recv):
        self.send, self.recv, self.made = send, recv, []

    def __call__(self, src, dst, device):
        i = len(self.made)
        copy = pltpu.make_async_remote_copy(
            src_ref=src,
            dst_ref=dst,
            send_sem=self.send.at[i],
            recv_sem=self.recv.at[i],
            device_id=device,
            device_id_type=MESH,
        )
        copy.start()
        self.made.append(copy)
        return copy

    def wait_sends(self):
        for copy in self.made:
            copy.wait_send()


def barrier(devices):
    sem = pltpu.get_barrier_semaphore()
    for device in devices:
        pl.semaphore_signal(sem, inc=1, device_id=device, device_id_type=MESH)
    pl.semaphore_wait(sem, len(devices))


def at(slot, rows, offset=0, count=None):
    return pl.ds(pl.multiple_of(slot * rows + offset, 16), rows if count is None else count)


def plane_ring(copies, p, src, where, rows):
    half = rows // 2
    right, left = p.xslot(1), p.xslot(-1)
    far = p.xslot(2)
    partner = p.in_plane(p.xslot(0, True))
    mine = where(p.slot, 0, rows)
    a = copies(src, mine, p.in_plane(right))
    b = copies(src, mine, p.in_plane(left))
    own = copies(src, mine, partner)
    yield
    a.wait_recv()
    first = where(left, 0, half)
    f = copies(first, first, p.in_plane(right))
    block = where(left, 0, rows)
    pa = copies(block, block, partner)
    b.wait_recv()
    second = where(right, half, half)
    g = copies(second, second, p.in_plane(left))
    block = where(right, 0, rows)
    pb = copies(block, block, partner)
    yield
    f.wait_recv()
    g.wait_recv()
    block = where(far, 0, rows)
    pc = copies(block, block, partner)
    yield
    own.wait_recv()
    pa.wait_recv()
    pb.wait_recv()
    pc.wait_recv()


def whole(ref, rows):
    return lambda slot, offset, count: ref.at[at(slot, rows, offset, count)]


def column_ring(copies, p, src, ref):
    def block(distance):
        return ref.at[at(place(distance), TOK)]

    up, down = p.in_column(p.zslot(1)), p.in_column(p.zslot(-1))
    u = copies(src, block(-1), up)
    d = copies(src, block(1), down)
    for step in range(1, Z // 2 + 1):
        yield
        u.wait_recv()
        if step < Z // 2:
            u = copies(block(-step), block(-step - 1), up)
        if step < Z // 2:
            d.wait_recv()
            if step < Z // 2 - 1:
                d = copies(block(step), block(step + 1), down)


def run(*rings):
    rings = list(rings)
    while rings:
        rings = [ring for ring in rings if next(ring, True) is None]


def plane_peers(p):
    return [p.in_plane(p.xslot(s, f)) for s in range(X) for f in (False, True) if s or f]


def column_peers(p):
    return [p.in_column(p.zslot(s)) for s in range(1, Z)]


def row_peers(p):
    return [{"fsdp": p.yslot(s)} for s in range(1, Y)]


def sum_squares(ref, chunk=64):
    width = ref.shape[1]

    def step(i, acc):
        block = ref[pl.ds(pl.multiple_of(i * chunk, chunk), chunk), :].astype(F32)
        return acc + jnp.sum((block * block).reshape(chunk // 8, 8, width), axis=0)

    acc = lax.fori_loop(0, ref.shape[0] // chunk, step, jnp.zeros((8, width), F32))
    return jnp.sum(acc, axis=0, keepdims=True)


def place(distance):
    return (distance + Z - 2) % Z


def sum_squares(ref, chunk=64):
    width = ref.shape[1]

    def step(i, acc):
        block = ref[pl.ds(pl.multiple_of(i * chunk, chunk), chunk), :].astype(F32)
        return acc + jnp.sum((block * block).reshape(chunk // 8, 8, width), axis=0)

    acc = lax.fori_loop(0, ref.shape[0] // chunk, step, jnp.zeros((8, width), F32))
    return jnp.sum(acc, axis=0, keepdims=True)


def build_bias(owners, pos, bias, p):
    lane = lax.broadcasted_iota(jnp.int32, (1, TOK), 1)
    low = lane < HALF
    row = lax.broadcasted_iota(jnp.int32, (HALF, TOK), 0)

    def step(slot, carry):
        owner = owners[p.z * G + slot]
        where = lane + jnp.where(low, owner * HALF, (2 * PAIRS - 1 - owner) * HALF - HALF)
        floor = where - pos[slot, 0:1, :]
        cols = pl.ds(pl.multiple_of(slot * TOK, TOK), TOK)
        for distance in range(Z):
            owner = owners[p.zslot(distance) * G + p.slot]
            for h, stretch in enumerate((owner, 2 * PAIRS - 1 - owner)):
                key = row + stretch * HALF
                seen = (key <= where) & (key >= floor)
                rows = pl.ds(place(distance) * TOK + h * HALF, HALF)
                bias[rows, cols] = jnp.where(seen, 0.0, NEGATIVE)
        return carry

    lax.fori_loop(0, G, step, 0)


def tile_of(t):
    return pl.ds(pl.multiple_of(t * TILE, TILE), TILE)


def tile_stats(qg, dog, kg, vg, bias, out, t):
    tile = tile_of(t)
    for h in range(HEADS):
        cols = pl.ds(h * DH, DH)
        raw = lax.dot_general(kg[...], qg[tile, cols], LAST, preferred_element_type=F32)
        raw = raw + bias[:, tile]
        top = jnp.max(raw, axis=0, keepdims=True)
        mass = jnp.exp2((raw - top) * SCALE2)
        total = jnp.sum(mass, axis=0, keepdims=True)
        dp = lax.dot_general(vg[...], dog[tile, cols], LAST, preferred_element_type=F32)
        dsum = jnp.sum(mass * dp, axis=0, keepdims=True)
        out[h : h + 1, tile] = top * SCALE2 + jnp.log2(total)
        out[HEADS + h : HEADS + h + 1, tile] = dsum / total


def merge_stats(shared, merged):
    for h in range(HEADS):
        parts = shared[:, h, :]
        top = jnp.max(parts, axis=0, keepdims=True)
        weight = jnp.exp2(parts - top)
        total = jnp.sum(weight, axis=0, keepdims=True)
        merged[h : h + 1, :] = top + jnp.log2(total)
        dsum = jnp.sum(weight * shared[:, HEADS + h, :], axis=0, keepdims=True)
        merged[HEADS + h : HEADS + h + 1, :] = dsum / total


def half_grads(qg, dog, kg, vg, kt, bias, merged, probs, slopes, acc, dqt, dq, dk, dv, half):
    count = kg.shape[0] // 2
    rows = pl.ds(half * count, count)
    acc[...] = jnp.zeros_like(acc)

    def step(t, carry):
        tile = tile_of(t)
        for h in range(HEADS):
            cols = pl.ds(h * DH, DH)
            wide = pl.ds(h * TILE, TILE)
            raw = lax.dot_general(kg[rows, :], qg[tile, cols], LAST, preferred_element_type=F32)
            prob = jnp.exp2((raw + bias[rows, tile]) * SCALE2 - merged[h : h + 1, tile])
            dp = lax.dot_general(vg[rows, :], dog[tile, cols], LAST, preferred_element_type=F32)
            slope = prob * (dp - merged[HEADS + h : HEADS + h + 1, tile])
            probs[:, wide] = prob.astype(BF16)
            slopes[:, wide] = slope.astype(BF16)
            part = jnp.dot(kt[:, rows], slopes[:, wide], preferred_element_type=F32)
            if half == 0:
                dqt[t, :, wide] = part
            else:
                dq[tile, cols] = ((part + dqt[t, :, wide]) * SCALE).T.astype(BF16)
        tall = lambda ref: jnp.concatenate(
            [ref[tile, pl.ds(h * DH, DH)] for h in range(HEADS)], axis=0
        )
        acc[:, :DH] += jnp.dot(slopes[...], tall(qg), preferred_element_type=F32)
        acc[:, DH:] += jnp.dot(probs[...], tall(dog), preferred_element_type=F32)
        return carry

    lax.fori_loop(0, qg.shape[0] // TILE, step, 0)
    dk[rows, :] = (acc[:, :DH] * SCALE).astype(BF16)
    dv[rows, :] = acc[:, DH:].astype(BF16)


FARTHEST = (4, 3, 5, 2, 6, 1, 7)


def rounded_sum(ref, i, count):
    total = ref[i, 0].astype(F32)
    for n in range(1, count):
        total = total + ref[i, n].astype(F32)
    return total.astype(BF16)


def kernel(
    owners, q, do, k, v, pos, hid, kw, vw, dq_slots, raw_k, raw_v, sums,
    qg, dog, kg, vg, pg, bias, shared, merged, kt, probs, slopes, acc, dqt, dq, dk, dv,
    hg, hgt, pq, cq, gz, gy, grads, part, rz, ysum, wsum, tw,
    send, recv, share_send, share_recv, local,
):
    p = Place()
    group = lax.div(p.y * HEADS, HPG)
    head_cols = pl.ds(pl.multiple_of(group * DH, DH), DH)
    own_k, own_v = k.at[:, head_cols], v.at[:, head_cols]
    wide = hid.shape[1] // G
    piece = wide // Z
    mine = at(p.slot, TOK)
    members = Y // KVG

    def strip(slot):
        return hid.at[:, pl.ds(pl.multiple_of(slot * wide, 128), wide)]

    moves = [
        (q, qg.at[mine]),
        (do, dog.at[mine]),
        (own_k, kg.at[at(place(0), TOK)]),
        (own_v, vg.at[at(place(0), TOK)]),
        (strip(p.slot), hg.at[mine]),
        (kw, tw.at[0]),
        (vw, tw.at[1]),
    ]
    loads = [pltpu.make_async_copy(s, d, local.at[i]) for i, (s, d) in enumerate(moves)]
    for load in loads:
        load.start()
    pg[p.slot] = jnp.broadcast_to(pos[...], (8, TOK))
    barrier(plane_peers(p) + column_peers(p) + row_peers(p))
    copies = Copies(send, recv)
    small = [copies(pg.at[p.slot], pg.at[p.slot], peer) for peer in plane_peers(p)]
    kr = column_ring(copies, p, own_k, kg)
    vr = column_ring(copies, p, own_v, vg)
    qr = plane_ring(copies, p, q, whole(qg, TOK), TOK)
    dr = plane_ring(copies, p, do, whole(dog, TOK), TOK)
    for ring in (kr, vr, qr, dr):
        next(ring)
    for ring in (kr, vr):
        next(ring)
    for copy in small:
        copy.wait_recv()
    build_bias(owners, pg, bias, p)
    for ring in (kr, vr, qr):
        next(ring)
    for i in range(2):
        loads[5 + i].wait()
        wsum[i] = jnp.broadcast_to(sum_squares(tw.at[i]), wsum.shape[1:])
    for ring in (kr, vr, dr, qr, kr, vr, dr):
        next(ring, None)
    hs = []
    for s, f in ((2, False), (2, True), (1, False), (3, False), (1, True), (3, True), (0, True)):
        to = p.xslot(s, f)
        hs.append(copies(strip(to), hg.at[mine], p.in_plane(to)))
    run(qr, dr)
    for load in loads[:5]:
        load.wait()
    kt[...] = kg[...].T
    peers = plane_peers(p)
    mine_stats = shared.at[p.slot]

    def share(t):
        block = shared.at[p.slot, :, tile_of(t)]
        return [
            pltpu.make_async_remote_copy(
                src_ref=block,
                dst_ref=block,
                send_sem=share_send.at[n, t],
                recv_sem=share_recv.at[n, t],
                device_id=peer,
                device_id_type=MESH,
            )
            for n, peer in enumerate(peers)
        ]

    def stats_step(t, carry):
        tile_stats(qg, dog, kg, vg, bias, mine_stats, t)
        for copy in share(t):
            copy.start()
        return carry

    tiles = qg.shape[0] // TILE
    lax.fori_loop(0, tiles, stats_step, 0)
    for t in range(tiles):
        for copy in share(t):
            copy.wait_recv()
            copy.wait_send()
    merge_stats(shared, merged)

    def scatter(half):
        near = {0: (4, 3, 5, 2), 1: (6, 1, 7)}[half]
        return [
            [
                copies(src.at[at(place(s), TOK)], gz.at[i, p.z], p.in_column(p.zslot(s)))
                for s in near
            ]
            for i, src in enumerate((dk, dv))
        ]

    halves = []
    for half in range(2):
        half_grads(
            qg, dog, kg, vg, kt, bias, merged, probs, slopes, acc, dqt, dq, dk, dv, half
        )
        halves.append(scatter(half))
    own_g = [
        pltpu.make_async_copy(src.at[at(place(0), TOK)], gz.at[i, p.z], local.at[7 + i])
        for i, src in enumerate((dk, dv))
    ]
    for load in own_g:
        load.start()

    def stream(i, raw):
        made = halves[0][i] + halves[1][i]
        own_g[i].wait()
        for copy in made:
            copy.wait_recv()
        gy[i, p.y] = rounded_sum(gz, i, Z)
        made = [copies(gy.at[i, p.y], gy.at[i, p.y], peer) for peer in row_peers(p)]
        yield
        for copy in made:
            copy.wait_recv()
        for g in range(KVG):
            total = gy[i, g * members].astype(F32)
            for n in range(1, members):
                total = total + gy[i, g * members + n].astype(F32)
            grads[i, mine, g * DH : (g + 1) * DH] = total.astype(BF16)
        ring = plane_ring(copies, p, grads.at[i, mine], whole(grads.at[i], TOK), TOK)
        for _ in ring:
            yield
        product = jnp.dot(hgt[...], grads[i], preferred_element_type=F32)
        part[i] = product.astype(BF16)
        rz[i, p.z] = part[i, at(p.z, piece), :]
        made = [
            copies(part.at[i, at(p.zslot(s), piece)], rz.at[i, p.z], p.in_column(p.zslot(s)))
            for s in FARTHEST
        ]
        yield
        for copy in made:
            copy.wait_recv()
        own = pl.ds(pl.multiple_of(p.slot * wide + p.z * piece, 16), piece)
        raw[own, :] = rounded_sum(rz, i, Z)
        made = [
            copies(raw.at[own], raw.at[own], p.in_column(p.zslot(s))) for s in FARTHEST
        ]
        yield
        for copy in made:
            copy.wait_recv()
        ring = plane_ring(copies, p, raw.at[at(p.slot, wide)], whole(raw, wide), wide)
        next(ring)
        square = sum_squares(raw.at[at(p.slot, wide)])
        row = lax.broadcasted_iota(jnp.int32, (8, square.shape[1]), 0)
        ysum[i, p.y] = jnp.where(row == 0, square, wsum[i])
        made = [copies(ysum.at[i, p.y], ysum.at[i, p.y], peer) for peer in row_peers(p)]
        yield
        next(ring)
        for copy in made:
            copy.wait_recv()
        total = ysum[i, 0]
        for n in range(1, Y):
            total = total + ysum[i, n]
        sums[i, p.slot] = total
        made = [copies(sums.at[i, p.slot], sums.at[i, p.slot], peer) for peer in plane_peers(p)]
        yield
        next(ring)
        yield
        for _ in ring:
            pass
        for copy in made:
            copy.wait_recv()

    partner = p.in_plane(p.xslot(0, True))
    given = [copies(dq.at[at(x * C + 1 - p.c, TOK)], pq.at[x], partner) for x in range(X)]
    for copy in hs:
        copy.wait_recv()
    hgt[...] = hg[...].T
    streams = [stream(0, raw_k), stream(1, raw_v)]
    for one in streams:
        next(one)
    for x in range(X):
        given[x].wait_recv()
        cq[x] = (dq[at(x * C + p.c, TOK), :].astype(F32) + pq[x].astype(F32)).astype(BF16)
    qs = []
    for s in (2, 1, 3):
        to = lax.rem(p.x + s, X)
        qs.append(copies(cq.at[to], dq_slots.at[p.x], p.in_plane(to * C + p.c)))
    dq_slots[p.x] = cq[p.x]
    run(*streams)
    for copy in qs:
        copy.wait_recv()
    copies.wait_sends()


def shape(dims, kind=BF16):
    return jax.ShapeDtypeStruct(dims, kind)


def dma(n):
    return pltpu.SemaphoreType.DMA((n,))


def local(
    queries, keys, values, out_grad, hidden, key_weight, value_weight, stretch_owner, positions
):
    width = queries.shape[1]
    model = hidden.shape[1]
    piece = model // G
    columns = KVG * DH
    dq_slots, raw_k, raw_v, sums = pl.pallas_call(
        kernel,
        out_shape=(
            shape((X, TOK, width)),
            shape((model, columns)),
            shape((model, columns)),
            shape((2, G, 8, columns), F32),
        ),
        in_specs=[SMEM] + [ANY] * 4 + [VMEM] + [ANY] * 3,
        out_specs=(VMEM,) * 4,
        scratch_shapes=[
            pltpu.VMEM((ROWS, width), BF16),
            pltpu.VMEM((ROWS, width), BF16),
            pltpu.VMEM((Z * TOK, DH), BF16),
            pltpu.VMEM((Z * TOK, DH), BF16),
            pltpu.VMEM((G, 8, TOK), jnp.int32),
            pltpu.VMEM((Z * TOK, ROWS), F32),
            pltpu.VMEM((G, 2 * HEADS, ROWS), F32),
            pltpu.VMEM((2 * HEADS, ROWS), F32),
            pltpu.VMEM((DH, Z * TOK), BF16),
            pltpu.VMEM((Z * TOK // 2, HEADS * TILE), BF16),
            pltpu.VMEM((Z * TOK // 2, HEADS * TILE), BF16),
            pltpu.VMEM((Z * TOK // 2, 2 * DH), F32),
            pltpu.VMEM((ROWS // TILE, DH, HEADS * TILE), F32),
            pltpu.VMEM((ROWS, width), BF16),
            pltpu.VMEM((Z * TOK, DH), BF16),
            pltpu.VMEM((Z * TOK, DH), BF16),
            pltpu.VMEM((ROWS, piece), BF16),
            pltpu.VMEM((piece, ROWS), BF16),
            pltpu.VMEM((X, TOK, width), BF16),
            pltpu.VMEM((X, TOK, width), BF16),
            pltpu.VMEM((2, Z, TOK, DH), BF16),
            pltpu.VMEM((2, Y, TOK, DH), BF16),
            pltpu.VMEM((2, ROWS, columns), BF16),
            pltpu.VMEM((2, piece, columns), BF16),
            pltpu.VMEM((2, Z, piece // Z, columns), BF16),
            pltpu.VMEM((2, Y, 8, columns), F32),
            pltpu.VMEM((2, 8, columns), F32),
            pltpu.VMEM((2, model, columns), BF16),
            dma(180),
            dma(180),
            pltpu.SemaphoreType.DMA((G - 1, ROWS // TILE)),
            pltpu.SemaphoreType.DMA((G - 1, ROWS // TILE)),
            dma(9),
        ],
        compiler_params=pltpu.CompilerParams(
            collective_id=0, has_side_effects=True, vmem_limit_bytes=VMEM_BYTES
        ),
    )(
        stretch_owner, queries, out_grad, keys, values, positions.reshape(1, TOK),
        hidden, key_weight, value_weight,
    )
    query_grad = jnp.sum(dq_slots.astype(F32), axis=0).astype(BF16)
    tokens = TOK * PAIRS

    def clipped(i, raw):
        grad_norm = jnp.sqrt(jnp.sum(sums[i, :, 0], axis=0) + EPSILON)
        weight_norm = jnp.sqrt(sums[i, 0, 1] + EPSILON)
        factor = jnp.minimum(1.0, CLIP_RATE * tokens * weight_norm / grad_norm)
        return raw.astype(F32) * factor[None, :]

    return (query_grad, clipped(0, raw_k), clipped(1, raw_v))


def solution(mesh):
    return jax.shard_map(
        local,
        mesh=mesh,
        in_specs=(
            P("ctx", "fsdp"),
            P("ctx", None),
            P("ctx", None),
            P("ctx", "fsdp"),
            P("ctx", "fsdp"),
            P("fsdp", None),
            P("fsdp", None),
            P(),
            P("ctx"),
        ),
        out_specs=(P("ctx", "fsdp"), P("fsdp", None), P("fsdp", None)),
        check_vma=False,
    )
```

```python
import functools
import math

import jax
import jax.numpy as jnp
from jax import lax
from jax.experimental import pallas as pl
from jax.experimental.pallas import tpu as pltpu
from jax.sharding import PartitionSpec as P

DH = 128
HPG = 8
KVG = 2
TOK = 128
HALF = TOK // 2
Z = 8
X = 4
C = 2
Y = 4
G = X * C
PAIRS = Z * X * C
HEADS = 4
ROWS = G * TOK
CLIP_RATE = 0.02
TILE = 256
VMEM_BYTES = 55 * 1024 * 1024
CHUNKS = 2
EPSILON = 1e-06
NEGATIVE = -1e30
SCALE = 1.0 / math.sqrt(DH)
SCALE2 = SCALE * math.log2(math.e)
MESH = pl.DeviceIdType.MESH
ANY = pl.BlockSpec(memory_space=pl.ANY)
VMEM = pl.BlockSpec(memory_space=pltpu.VMEM)
HBM = pl.BlockSpec(memory_space=pltpu.HBM)
SMEM = pl.BlockSpec(memory_space=pltpu.SMEM)
LAST = (((1,), (1,)), ((), ()))
FIRST = (((0,), (0,)), ((), ()))
BF16 = jnp.bfloat16
F32 = jnp.float32


class Place:
    def __init__(self):
        me = lax.axis_index("ctx")
        self.me = me
        self.y = lax.axis_index("fsdp")
        self.z = lax.div(me, G)
        self.slot = lax.rem(me, G)
        self.x = lax.div(self.slot, C)
        self.c = lax.rem(self.slot, C)

    def xslot(self, step, flip=False):
        x = lax.rem(self.x + step + X, X)
        return x * C + ((1 - self.c) if flip else self.c)

    def in_plane(self, slot):
        return {"ctx": self.z * G + slot}

    def zslot(self, step):
        return lax.rem(self.z + step + Z, Z)

    def in_column(self, z):
        return {"ctx": z * G + self.slot}

    def yslot(self, step):
        return lax.rem(self.y + step, Y)


class Copies:
    def __init__(self, send, recv):
        self.send, self.recv, self.made = send, recv, []

    def __call__(self, src, dst, device):
        i = len(self.made)
        copy = pltpu.make_async_remote_copy(
            src_ref=src,
            dst_ref=dst,
            send_sem=self.send.at[i],
            recv_sem=self.recv.at[i],
            device_id=device,
            device_id_type=MESH,
        )
        copy.start()
        self.made.append(copy)
        return copy

    def wait_sends(self):
        for copy in self.made:
            copy.wait_send()


def greet(devices):
    for device in devices:
        pl.semaphore_signal(
            pltpu.get_barrier_semaphore(), inc=1, device_id=device, device_id_type=MESH
        )


def meet(devices):
    pl.semaphore_wait(pltpu.get_barrier_semaphore(), len(devices))


def at(slot, rows, offset=0, count=None):
    return pl.ds(pl.multiple_of(slot * rows + offset, 16), rows if count is None else count)


def plane_ring(copies, p, src, where, rows):
    half = rows // 2
    right, left = p.xslot(1), p.xslot(-1)
    far = p.xslot(2)
    partner = p.in_plane(p.xslot(0, True))
    mine = where(p.slot, 0, rows)
    a = copies(src, mine, p.in_plane(right))
    b = copies(src, mine, p.in_plane(left))
    own = copies(src, mine, partner)
    yield
    a.wait_recv()
    first = where(left, 0, half)
    f = copies(first, first, p.in_plane(right))
    block = where(left, 0, rows)
    pa = copies(block, block, partner)
    b.wait_recv()
    second = where(right, half, half)
    g = copies(second, second, p.in_plane(left))
    block = where(right, 0, rows)
    pb = copies(block, block, partner)
    yield
    f.wait_recv()
    g.wait_recv()
    block = where(far, 0, rows)
    pc = copies(block, block, partner)
    yield
    own.wait_recv()
    pa.wait_recv()
    pb.wait_recv()
    pc.wait_recv()


def whole(ref, rows):
    return lambda slot, offset, count: ref.at[at(slot, rows, offset, count)]


def column_ring(copies, p, src, ref):
    def block(distance):
        return ref.at[at(place(distance), TOK)]

    up, down = p.in_column(p.zslot(1)), p.in_column(p.zslot(-1))
    u = copies(src, block(-1), up)
    d = copies(src, block(1), down)
    for step in range(1, Z // 2 + 1):
        yield
        u.wait_recv()
        if step < Z // 2:
            u = copies(block(-step), block(-step - 1), up)
        if step < Z // 2:
            d.wait_recv()
            if step < Z // 2 - 1:
                d = copies(block(step), block(step + 1), down)


def run(*rings):
    rings = list(rings)
    while rings:
        rings = [ring for ring in rings if next(ring, True) is None]


def plane_peers(p):
    return [p.in_plane(p.xslot(s, f)) for s in range(X) for f in (False, True) if s or f]


def column_peers(p):
    return [p.in_column(p.zslot(s)) for s in range(1, Z)]


def row_peers(p):
    return [{"fsdp": p.yslot(s)} for s in range(1, Y)]


def sum_squares(ref, chunk=64):
    width = ref.shape[1]

    def step(i, acc):
        block = ref[pl.ds(pl.multiple_of(i * chunk, chunk), chunk), :].astype(F32)
        return acc + jnp.sum((block * block).reshape(chunk // 8, 8, width), axis=0)

    acc = lax.fori_loop(0, ref.shape[0] // chunk, step, jnp.zeros((8, width), F32))
    return jnp.sum(acc, axis=0, keepdims=True)


def place(distance):
    return (distance + Z - 2) % Z


def sum_squares(ref, chunk=64):
    width = ref.shape[1]

    def step(i, acc):
        block = ref[pl.ds(pl.multiple_of(i * chunk, chunk), chunk), :].astype(F32)
        return acc + jnp.sum((block * block).reshape(chunk // 8, 8, width), axis=0)

    acc = lax.fori_loop(0, ref.shape[0] // chunk, step, jnp.zeros((8, width), F32))
    return jnp.sum(acc, axis=0, keepdims=True)


def build_bias(owners, pos, bias, p):
    lane = lax.broadcasted_iota(jnp.int32, (1, TOK), 1)
    low = lane < HALF
    row = lax.broadcasted_iota(jnp.int32, (HALF, TOK), 0)

    def step(slot, carry):
        owner = owners[p.z * G + slot]
        where = lane + jnp.where(low, owner * HALF, (2 * PAIRS - 1 - owner) * HALF - HALF)
        floor = where - pos[slot, 0:1, :]
        cols = pl.ds(pl.multiple_of(slot * TOK, TOK), TOK)
        for distance in range(Z):
            owner = owners[p.zslot(distance) * G + p.slot]
            for h, stretch in enumerate((owner, 2 * PAIRS - 1 - owner)):
                key = row + stretch * HALF
                seen = (key <= where) & (key >= floor)
                rows = pl.ds(place(distance) * TOK + h * HALF, HALF)
                bias[rows, cols] = jnp.where(seen, 0.0, NEGATIVE)
        return carry

    lax.fori_loop(0, G, step, 0)


def tile_of(t):
    return pl.ds(pl.multiple_of(t * TILE, TILE), TILE)


def head_of(t, h):
    return pl.ds(pl.multiple_of((t * HEADS + h) * TILE, TILE), TILE)


def tile_stats(qg, dog, kg, vg, bias, masses, dps, tops, out, t):
    tile = tile_of(t)
    for h in range(HEADS):
        cols = pl.ds(h * DH, DH)
        raw = lax.dot_general(kg[...], qg[tile, cols], LAST, preferred_element_type=F32)
        raw = raw + bias[:, tile]
        top = jnp.max(raw, axis=0, keepdims=True)
        mass = jnp.exp2((raw - top) * SCALE2)
        total = jnp.sum(mass, axis=0, keepdims=True)
        masses[:, head_of(t, h)] = mass.astype(BF16)
        dp = lax.dot_general(vg[...], dog[tile, cols], LAST, preferred_element_type=F32)
        dps[:, head_of(t, h)] = dp
        dsum = jnp.sum(mass * dp, axis=0, keepdims=True)
        tops[h : h + 1, tile] = top * SCALE2
        out[h : h + 1, tile] = top * SCALE2 + jnp.log2(total)
        out[HEADS + h : HEADS + h + 1, tile] = dsum / total


def merge_stats(shared, tops, merged, t):
    tile = tile_of(t)
    for h in range(HEADS):
        parts = shared[:, h, tile]
        top = jnp.max(parts, axis=0, keepdims=True)
        weight = jnp.exp2(parts - top)
        total = jnp.sum(weight, axis=0, keepdims=True)
        merged[h : h + 1, tile] = jnp.exp2(tops[h : h + 1, tile] - (top + jnp.log2(total)))
        dsum = jnp.sum(weight * shared[:, HEADS + h, tile], axis=0, keepdims=True)
        merged[HEADS + h : HEADS + h + 1, tile] = dsum / total


def chunk_grads(
    qg, dog, kt, masses, dps, merged, probs, slopes, acc, dqt, dq, dk, dv, chunk, ready
):
    count = masses.shape[0] // CHUNKS
    rows = pl.ds(chunk * count, count)
    acc[...] = jnp.zeros_like(acc)

    def step(t, carry):
        ready(t)
        tile = tile_of(t)
        for h in range(HEADS):
            cols = pl.ds(h * DH, DH)
            wide = pl.ds(h * TILE, TILE)
            prob = masses[rows, head_of(t, h)].astype(F32) * merged[h : h + 1, tile]
            slope = prob * (dps[rows, head_of(t, h)] - merged[HEADS + h : HEADS + h + 1, tile])
            probs[:, wide] = prob.astype(BF16)
            slopes[:, wide] = slope.astype(BF16)
            part = jnp.dot(kt[:, rows], slopes[:, wide], preferred_element_type=F32)
            if chunk > 0:
                part = part + dqt[t, :, wide]
            if chunk < CHUNKS - 1:
                dqt[t, :, wide] = part
            else:
                dq[tile, cols] = (part * SCALE).T.astype(BF16)
        tall = lambda ref: jnp.concatenate(
            [ref[tile, pl.ds(h * DH, DH)] for h in range(HEADS)], axis=0
        )
        acc[:, :DH] += jnp.dot(slopes[...], tall(qg), preferred_element_type=F32)
        acc[:, DH:] += jnp.dot(probs[...], tall(dog), preferred_element_type=F32)
        return carry

    lax.fori_loop(0, qg.shape[0] // TILE, step, 0)
    dk[rows, :] = (acc[:, :DH] * SCALE).astype(BF16)
    dv[rows, :] = acc[:, DH:].astype(BF16)


FARTHEST = (4, 3, 5, 2, 6, 1, 7)


def rounded_sum(ref, i, count):
    total = ref[i, 0].astype(F32)
    for n in range(1, count):
        total = total + ref[i, n].astype(F32)
    return total.astype(BF16)


def kernel(
    owners, q, do, k, v, pos, hid, kw, vw, dq_slots, raw_k, raw_v, sums,
    qg, dog, kg, vg, pg, bias, shared, merged, kt, masses, dps, tops, probs, slopes, acc, dqt, dq, dk, dv,
    hg, hgt, pq, cq, gz, gy, grads, part, rz, ysum, wsum, tw,
    send, recv, share_send, share_recv, local,
):
    p = Place()
    group = lax.div(p.y * HEADS, HPG)
    head_cols = pl.ds(pl.multiple_of(group * DH, DH), DH)
    own_k, own_v = k.at[:, head_cols], v.at[:, head_cols]
    wide = hid.shape[1] // G
    piece = wide // Z
    mine = at(p.slot, TOK)
    members = Y // KVG

    def strip(slot):
        return hid.at[:, pl.ds(pl.multiple_of(slot * wide, 128), wide)]

    moves = [
        (q, qg.at[mine]),
        (do, dog.at[mine]),
        (own_k, kg.at[at(place(0), TOK)]),
        (own_v, vg.at[at(place(0), TOK)]),
        (strip(p.slot), hg.at[mine]),
        (kw, tw.at[0]),
        (vw, tw.at[1]),
    ]
    everyone = plane_peers(p) + column_peers(p) + row_peers(p)
    greet(everyone)
    loads = [pltpu.make_async_copy(s, d, local.at[i]) for i, (s, d) in enumerate(moves)]
    for load in loads[5:] + loads[:5]:
        load.start()
    pg[p.slot] = jnp.broadcast_to(pos[...], (8, TOK))
    for i in range(2):
        loads[5 + i].wait()
        wsum[i] = jnp.broadcast_to(sum_squares(tw.at[i]), wsum.shape[1:])
    meet(everyone)
    copies = Copies(send, recv)
    small = [copies(pg.at[p.slot], pg.at[p.slot], peer) for peer in plane_peers(p)]
    kr = column_ring(copies, p, own_k, kg)
    vr = column_ring(copies, p, own_v, vg)
    qr = plane_ring(copies, p, q, whole(qg, TOK), TOK)
    dr = plane_ring(copies, p, do, whole(dog, TOK), TOK)
    for ring in (kr, vr, qr, dr):
        next(ring)
    for ring in (kr, vr):
        next(ring)
    for copy in small:
        copy.wait_recv()
    build_bias(owners, pg, bias, p)
    for ring in (kr, vr, qr):
        next(ring)
    for ring in (kr, vr, dr, qr, kr, vr, dr):
        next(ring, None)
    run(qr, dr)
    hs = []
    for s, f in ((2, False), (2, True), (1, False), (3, False), (1, True), (3, True), (0, True)):
        to = p.xslot(s, f)
        hs.append(copies(strip(to), hg.at[mine], p.in_plane(to)))
    for load in loads[:5]:
        load.wait()
    kt[...] = kg[...].T
    peers = plane_peers(p)
    mine_stats = shared.at[p.slot]

    def share(t):
        block = shared.at[p.slot, :, tile_of(t)]
        return [
            pltpu.make_async_remote_copy(
                src_ref=block,
                dst_ref=block,
                send_sem=share_send.at[n, t],
                recv_sem=share_recv.at[n, t],
                device_id=peer,
                device_id_type=MESH,
            )
            for n, peer in enumerate(peers)
        ]

    def stats_step(t, carry):
        tile_stats(qg, dog, kg, vg, bias, masses, dps, tops, mine_stats, t)
        for copy in share(t):
            copy.start()
        return carry

    tiles = qg.shape[0] // TILE
    lax.fori_loop(0, tiles, stats_step, 0)

    def ready(t):
        for copy in share(t):
            copy.wait_recv()
        merge_stats(shared, tops, merged, t)

    def scatter(chunk):
        count = Z // CHUNKS
        near = [s for s in FARTHEST if place(s) // count == chunk]
        return [
            [
                copies(src.at[at(place(s), TOK)], gz.at[i, p.z], p.in_column(p.zslot(s)))
                for s in near
            ]
            for i, src in enumerate((dk, dv))
        ]

    chunks = []
    for chunk in range(CHUNKS):
        chunk_grads(
            qg, dog, kt, masses, dps, merged, probs, slopes, acc, dqt, dq, dk, dv, chunk,
            ready if chunk == 0 else lambda t: None,
        )
        chunks.append(scatter(chunk))
    own_g = [
        pltpu.make_async_copy(src.at[at(place(0), TOK)], gz.at[i, p.z], local.at[7 + i])
        for i, src in enumerate((dk, dv))
    ]
    for load in own_g:
        load.start()

    def stream(i, raw):
        made = [copy for parts in chunks for copy in parts[i]]
        own_g[i].wait()
        for copy in made:
            copy.wait_recv()
        gy[i, p.y] = rounded_sum(gz, i, Z)
        made = [copies(gy.at[i, p.y], gy.at[i, p.y], peer) for peer in row_peers(p)]
        yield
        for copy in made:
            copy.wait_recv()
        for g in range(KVG):
            total = gy[i, g * members].astype(F32)
            for n in range(1, members):
                total = total + gy[i, g * members + n].astype(F32)
            grads[i, mine, g * DH : (g + 1) * DH] = total.astype(BF16)
        ring = plane_ring(copies, p, grads.at[i, mine], whole(grads.at[i], TOK), TOK)
        for _ in ring:
            yield
        product = jnp.dot(hgt[...], grads[i], preferred_element_type=F32)
        part[i] = product.astype(BF16)
        rz[i, p.z] = part[i, at(p.z, piece), :]
        made = [
            copies(part.at[i, at(p.zslot(s), piece)], rz.at[i, p.z], p.in_column(p.zslot(s)))
            for s in FARTHEST
        ]
        yield
        for copy in made:
            copy.wait_recv()
        own = pl.ds(pl.multiple_of(p.slot * wide + p.z * piece, 16), piece)
        raw[own, :] = rounded_sum(rz, i, Z)
        made = [
            copies(raw.at[own], raw.at[own], p.in_column(p.zslot(s))) for s in FARTHEST
        ]
        yield
        for copy in made:
            copy.wait_recv()
        ring = plane_ring(copies, p, raw.at[at(p.slot, wide)], whole(raw, wide), wide)
        next(ring)
        square = sum_squares(raw.at[at(p.slot, wide)])
        row = lax.broadcasted_iota(jnp.int32, (8, square.shape[1]), 0)
        ysum[i, p.y] = jnp.where(row == 0, square, wsum[i])
        made = [copies(ysum.at[i, p.y], ysum.at[i, p.y], peer) for peer in row_peers(p)]
        yield
        next(ring)
        for copy in made:
            copy.wait_recv()
        total = ysum[i, 0]
        for n in range(1, Y):
            total = total + ysum[i, n]
        sums[i, p.slot] = total
        made = [copies(sums.at[i, p.slot], sums.at[i, p.slot], peer) for peer in plane_peers(p)]
        yield
        next(ring)
        yield
        for _ in ring:
            pass
        for copy in made:
            copy.wait_recv()

    partner = p.in_plane(p.xslot(0, True))
    given = [copies(dq.at[at(x * C + 1 - p.c, TOK)], pq.at[x], partner) for x in range(X)]
    for copy in hs:
        copy.wait_recv()
    hgt[...] = hg[...].T
    streams = [stream(0, raw_k), stream(1, raw_v)]
    for one in streams:
        next(one)
    for x in range(X):
        given[x].wait_recv()
        cq[x] = (dq[at(x * C + p.c, TOK), :].astype(F32) + pq[x].astype(F32)).astype(BF16)
    qs = []
    for s in (2, 1, 3):
        to = lax.rem(p.x + s, X)
        qs.append(copies(cq.at[to], dq_slots.at[p.x], p.in_plane(to * C + p.c)))
    dq_slots[p.x] = cq[p.x]
    run(*streams)
    for copy in qs:
        copy.wait_recv()
    copies.wait_sends()
    for t in range(tiles):
        for copy in share(t):
            copy.wait_send()


def shape(dims, kind=BF16):
    return jax.ShapeDtypeStruct(dims, kind)


def dma(n):
    return pltpu.SemaphoreType.DMA((n,))


def local(
    queries, keys, values, out_grad, hidden, key_weight, value_weight, stretch_owner, positions
):
    width = queries.shape[1]
    model = hidden.shape[1]
    piece = model // G
    columns = KVG * DH
    dq_slots, raw_k, raw_v, sums = pl.pallas_call(
        kernel,
        out_shape=(
            pltpu.VMEM((X, TOK, width), BF16),
            pltpu.VMEM((model, columns), BF16),
            pltpu.VMEM((model, columns), BF16),
            pltpu.VMEM((2, G, 8, columns), F32),
        ),
        in_specs=[SMEM] + [ANY] * 4 + [VMEM] + [ANY] * 3,
        out_specs=(VMEM,) * 4,
        scratch_shapes=[
            pltpu.VMEM((ROWS, width), BF16),
            pltpu.VMEM((ROWS, width), BF16),
            pltpu.VMEM((Z * TOK, DH), BF16),
            pltpu.VMEM((Z * TOK, DH), BF16),
            pltpu.VMEM((G, 8, TOK), jnp.int32),
            pltpu.VMEM((Z * TOK, ROWS), F32),
            pltpu.VMEM((G, 2 * HEADS, ROWS), F32),
            pltpu.VMEM((2 * HEADS, ROWS), F32),
            pltpu.VMEM((DH, Z * TOK), BF16),
            pltpu.VMEM((Z * TOK, HEADS * ROWS), BF16),
            pltpu.VMEM((Z * TOK, HEADS * ROWS), F32),
            pltpu.VMEM((8, ROWS), F32),
            pltpu.VMEM((Z * TOK // CHUNKS, HEADS * TILE), BF16),
            pltpu.VMEM((Z * TOK // CHUNKS, HEADS * TILE), BF16),
            pltpu.VMEM((Z * TOK // CHUNKS, 2 * DH), F32),
            pltpu.VMEM((ROWS // TILE, DH, HEADS * TILE), F32),
            pltpu.VMEM((ROWS, width), BF16),
            pltpu.VMEM((Z * TOK, DH), BF16),
            pltpu.VMEM((Z * TOK, DH), BF16),
            pltpu.VMEM((ROWS, piece), BF16),
            pltpu.VMEM((piece, ROWS), BF16),
            pltpu.VMEM((X, TOK, width), BF16),
            pltpu.VMEM((X, TOK, width), BF16),
            pltpu.VMEM((2, Z, TOK, DH), BF16),
            pltpu.VMEM((2, Y, TOK, DH), BF16),
            pltpu.VMEM((2, ROWS, columns), BF16),
            pltpu.VMEM((2, piece, columns), BF16),
            pltpu.VMEM((2, Z, piece // Z, columns), BF16),
            pltpu.VMEM((2, Y, 8, columns), F32),
            pltpu.VMEM((2, 8, columns), F32),
            pltpu.VMEM((2, model, columns), BF16),
            dma(180),
            dma(180),
            pltpu.SemaphoreType.DMA((G - 1, ROWS // TILE)),
            pltpu.SemaphoreType.DMA((G - 1, ROWS // TILE)),
            dma(9),
        ],
        compiler_params=pltpu.CompilerParams(
            collective_id=0, has_side_effects=True, vmem_limit_bytes=VMEM_BYTES
        ),
    )(
        stretch_owner, queries, out_grad, keys, values, positions.reshape(1, TOK),
        hidden, key_weight, value_weight,
    )
    query_grad = jnp.sum(dq_slots.astype(F32), axis=0).astype(BF16)
    tokens = TOK * PAIRS

    def clipped(i, raw):
        grad_norm = jnp.sqrt(jnp.sum(sums[i, :, 0], axis=0) + EPSILON)
        weight_norm = jnp.sqrt(sums[i, 0, 1] + EPSILON)
        factor = jnp.minimum(1.0, CLIP_RATE * tokens * weight_norm / grad_norm)
        return raw.astype(F32) * factor[None, :]

    return (query_grad, clipped(0, raw_k), clipped(1, raw_v))


def solution(mesh):
    return jax.shard_map(
        local,
        mesh=mesh,
        in_specs=(
            P("ctx", "fsdp"),
            P("ctx", None),
            P("ctx", None),
            P("ctx", "fsdp"),
            P("ctx", "fsdp"),
            P("fsdp", None),
            P("fsdp", None),
            P(),
            P("ctx"),
        ),
        out_specs=(P("ctx", "fsdp"), P("fsdp", None), P("fsdp", None)),
        check_vma=False,
    )
```

```python
import functools
import math

import jax
import jax.numpy as jnp
from jax import lax
from jax.experimental import pallas as pl
from jax.experimental.pallas import tpu as pltpu
from jax.sharding import PartitionSpec as P

DH = 128
HPG = 8
KVG = 2
TOK = 128
HALF = TOK // 2
Z = 8
X = 4
C = 2
Y = 4
G = X * C
PAIRS = Z * X * C
HEADS = 4
ROWS = G * TOK
CLIP_RATE = 0.02
TILE = 256
VMEM_BYTES = 55 * 1024 * 1024
CHUNKS = 4
ORDER = (3, 5, 4, 2, 6, 1, 7, 0)
EPSILON = 1e-06
NEGATIVE = -1e30
SCALE = 1.0 / math.sqrt(DH)
SCALE2 = SCALE * math.log2(math.e)
MESH = pl.DeviceIdType.MESH
ANY = pl.BlockSpec(memory_space=pl.ANY)
VMEM = pl.BlockSpec(memory_space=pltpu.VMEM)
HBM = pl.BlockSpec(memory_space=pltpu.HBM)
SMEM = pl.BlockSpec(memory_space=pltpu.SMEM)
LAST = (((1,), (1,)), ((), ()))
FIRST = (((0,), (0,)), ((), ()))
BF16 = jnp.bfloat16
F32 = jnp.float32


class Place:
    def __init__(self):
        me = lax.axis_index("ctx")
        self.me = me
        self.y = lax.axis_index("fsdp")
        self.z = lax.div(me, G)
        self.slot = lax.rem(me, G)
        self.x = lax.div(self.slot, C)
        self.c = lax.rem(self.slot, C)

    def xslot(self, step, flip=False):
        x = lax.rem(self.x + step + X, X)
        return x * C + ((1 - self.c) if flip else self.c)

    def in_plane(self, slot):
        return {"ctx": self.z * G + slot}

    def zslot(self, step):
        return lax.rem(self.z + step + Z, Z)

    def in_column(self, z):
        return {"ctx": z * G + self.slot}

    def yslot(self, step):
        return lax.rem(self.y + step, Y)


class Copies:
    def __init__(self, send, recv):
        self.send, self.recv, self.made = send, recv, []

    def __call__(self, src, dst, device):
        i = len(self.made)
        copy = pltpu.make_async_remote_copy(
            src_ref=src,
            dst_ref=dst,
            send_sem=self.send.at[i],
            recv_sem=self.recv.at[i],
            device_id=device,
            device_id_type=MESH,
        )
        copy.start()
        self.made.append(copy)
        return copy

    def wait_sends(self):
        for copy in self.made:
            copy.wait_send()


def greet(devices):
    for device in devices:
        pl.semaphore_signal(
            pltpu.get_barrier_semaphore(), inc=1, device_id=device, device_id_type=MESH
        )


def meet(devices):
    pl.semaphore_wait(pltpu.get_barrier_semaphore(), len(devices))


def at(slot, rows, offset=0, count=None):
    return pl.ds(pl.multiple_of(slot * rows + offset, 16), rows if count is None else count)


def plane_ring(copies, p, src, where, rows):
    half = rows // 2
    right, left = p.xslot(1), p.xslot(-1)
    far = p.xslot(2)
    partner = p.in_plane(p.xslot(0, True))
    mine = where(p.slot, 0, rows)
    a = copies(src, mine, p.in_plane(right))
    b = copies(src, mine, p.in_plane(left))
    own = copies(src, mine, partner)
    yield
    a.wait_recv()
    first = where(left, 0, half)
    f = copies(first, first, p.in_plane(right))
    block = where(left, 0, rows)
    pa = copies(block, block, partner)
    b.wait_recv()
    second = where(right, half, half)
    g = copies(second, second, p.in_plane(left))
    block = where(right, 0, rows)
    pb = copies(block, block, partner)
    yield
    f.wait_recv()
    g.wait_recv()
    block = where(far, 0, rows)
    pc = copies(block, block, partner)
    yield
    own.wait_recv()
    pa.wait_recv()
    pb.wait_recv()
    pc.wait_recv()


def plane_direct(copies, p, src, where, rows):
    partner = p.in_plane(p.xslot(0, True))
    mine = where(p.slot, 0, rows)
    c, a, b = [copies(src, mine, p.in_plane(p.xslot(s))) for s in (2, 1, -1)]
    passed = [copies(src, mine, partner)]
    yield
    for copy, s in ((a, -1), (b, 1)):
        copy.wait_recv()
        block = where(p.xslot(s), 0, rows)
        passed.append(copies(block, block, partner))
    yield
    c.wait_recv()
    block = where(p.xslot(2), 0, rows)
    passed.append(copies(block, block, partner))
    yield
    for copy in passed:
        copy.wait_recv()


def whole(ref, rows):
    return lambda slot, offset, count: ref.at[at(slot, rows, offset, count)]


def column_ring(copies, p, src, ref):
    def block(distance):
        return ref.at[at(place(distance), TOK)]

    up, down = p.in_column(p.zslot(1)), p.in_column(p.zslot(-1))
    u = copies(src, block(-1), up)
    d = copies(src, block(1), down)
    for step in range(1, Z // 2 + 1):
        yield
        u.wait_recv()
        if step < Z // 2:
            u = copies(block(-step), block(-step - 1), up)
        if step < Z // 2:
            d.wait_recv()
            if step < Z // 2 - 1:
                d = copies(block(step), block(step + 1), down)


def run(*rings):
    rings = list(rings)
    while rings:
        rings = [ring for ring in rings if next(ring, True) is None]


def plane_peers(p):
    return [p.in_plane(p.xslot(s, f)) for s in range(X) for f in (False, True) if s or f]


def column_peers(p):
    return [p.in_column(p.zslot(s)) for s in range(1, Z)]


def row_peers(p):
    return [{"fsdp": p.yslot(s)} for s in range(1, Y)]


def sum_squares(ref, chunk=64):
    width = ref.shape[1]

    def step(i, acc):
        block = ref[pl.ds(pl.multiple_of(i * chunk, chunk), chunk), :].astype(F32)
        return acc + jnp.sum((block * block).reshape(chunk // 8, 8, width), axis=0)

    acc = lax.fori_loop(0, ref.shape[0] // chunk, step, jnp.zeros((8, width), F32))
    return jnp.sum(acc, axis=0, keepdims=True)


def place(distance):
    return ORDER.index(distance % Z)


def sum_squares(ref, chunk=64):
    width = ref.shape[1]

    def step(i, acc):
        block = ref[pl.ds(pl.multiple_of(i * chunk, chunk), chunk), :].astype(F32)
        return acc + jnp.sum((block * block).reshape(chunk // 8, 8, width), axis=0)

    acc = lax.fori_loop(0, ref.shape[0] // chunk, step, jnp.zeros((8, width), F32))
    return jnp.sum(acc, axis=0, keepdims=True)


def build_bias(owners, pos, bias, p):
    lane = lax.broadcasted_iota(jnp.int32, (1, TOK), 1)
    low = lane < HALF
    row = lax.broadcasted_iota(jnp.int32, (HALF, TOK), 0)

    def step(slot, carry):
        owner = owners[p.z * G + slot]
        where = lane + jnp.where(low, owner * HALF, (2 * PAIRS - 1 - owner) * HALF - HALF)
        floor = where - pos[slot, 0:1, :]
        cols = pl.ds(pl.multiple_of(slot * TOK, TOK), TOK)
        for distance in range(Z):
            owner = owners[p.zslot(distance) * G + p.slot]
            for h, stretch in enumerate((owner, 2 * PAIRS - 1 - owner)):
                key = row + stretch * HALF
                seen = (key <= where) & (key >= floor)
                rows = pl.ds(place(distance) * TOK + h * HALF, HALF)
                bias[rows, cols] = jnp.where(seen, 0.0, NEGATIVE)
        return carry

    lax.fori_loop(0, G, step, 0)


def tile_of(t):
    return pl.ds(pl.multiple_of(t * TILE, TILE), TILE)


def head_of(t, h):
    return pl.ds(pl.multiple_of((t * HEADS + h) * TILE, TILE), TILE)


def tile_stats(qg, dog, kg, vg, bias, masses, dps, tops, out, t):
    tile = tile_of(t)
    for h in range(HEADS):
        cols = pl.ds(h * DH, DH)
        raw = lax.dot_general(kg[...], qg[tile, cols], LAST, preferred_element_type=F32)
        raw = raw + bias[:, tile]
        top = jnp.max(raw, axis=0, keepdims=True)
        mass = jnp.exp2((raw - top) * SCALE2)
        total = jnp.sum(mass, axis=0, keepdims=True)
        masses[:, head_of(t, h)] = mass.astype(BF16)
        dp = lax.dot_general(vg[...], dog[tile, cols], LAST, preferred_element_type=F32)
        dps[:, head_of(t, h)] = dp
        dsum = jnp.sum(mass * dp, axis=0, keepdims=True)
        tops[h : h + 1, tile] = top * SCALE2
        out[h : h + 1, tile] = top * SCALE2 + jnp.log2(total)
        out[HEADS + h : HEADS + h + 1, tile] = dsum / total


def merge_stats(shared, tops, merged, t):
    tile = tile_of(t)
    for h in range(HEADS):
        parts = shared[:, h, tile]
        top = jnp.max(parts, axis=0, keepdims=True)
        weight = jnp.exp2(parts - top)
        total = jnp.sum(weight, axis=0, keepdims=True)
        merged[h : h + 1, tile] = jnp.exp2(tops[h : h + 1, tile] - (top + jnp.log2(total)))
        dsum = jnp.sum(weight * shared[:, HEADS + h, tile], axis=0, keepdims=True)
        merged[HEADS + h : HEADS + h + 1, tile] = dsum / total


def chunk_grads(
    qg, dog, kt, masses, dps, merged, probs, slopes, acc, dqt, dq, dk, dv, chunk, ready
):
    count = masses.shape[0] // CHUNKS
    rows = pl.ds(chunk * count, count)
    acc[...] = jnp.zeros_like(acc)

    def step(t, carry):
        ready(t)
        tile = tile_of(t)
        for h in range(HEADS):
            cols = pl.ds(h * DH, DH)
            wide = pl.ds(h * TILE, TILE)
            prob = masses[rows, head_of(t, h)].astype(F32) * merged[h : h + 1, tile]
            slope = prob * (dps[rows, head_of(t, h)] - merged[HEADS + h : HEADS + h + 1, tile])
            probs[:, wide] = prob.astype(BF16)
            slopes[:, wide] = slope.astype(BF16)
            part = jnp.dot(kt[:, rows], slopes[:, wide], preferred_element_type=F32)
            if chunk > 0:
                part = part + dqt[t, :, wide]
            if chunk < CHUNKS - 1:
                dqt[t, :, wide] = part
            else:
                dq[tile, cols] = (part * SCALE).T.astype(BF16)
        tall = lambda ref: jnp.concatenate(
            [ref[tile, pl.ds(h * DH, DH)] for h in range(HEADS)], axis=0
        )
        acc[:, :DH] += jnp.dot(slopes[...], tall(qg), preferred_element_type=F32)
        acc[:, DH:] += jnp.dot(probs[...], tall(dog), preferred_element_type=F32)
        return carry

    lax.fori_loop(0, qg.shape[0] // TILE, step, 0)
    dk[rows, :] = (acc[:, :DH] * SCALE).astype(BF16)
    dv[rows, :] = acc[:, DH:].astype(BF16)


FARTHEST = (4, 3, 5, 2, 6, 1, 7)


def rounded_sum(ref, i, count):
    total = ref[i, 0].astype(F32)
    for n in range(1, count):
        total = total + ref[i, n].astype(F32)
    return total.astype(BF16)


def kernel(
    owners, q, do, k, v, pos, hid, kw, vw, dq_slots, raw_k, raw_v, sums,
    qg, dog, kg, vg, pg, bias, shared, merged, kt, masses, dps, tops, probs, slopes, acc, dqt, dq, dk, dv,
    hg, hgt, pq, cq, gz, gy, grads, part, rz, ysum, wsum, tw, block, tot,
    send, recv, share_send, share_recv, local,
):
    p = Place()
    group = lax.div(p.y * HEADS, HPG)
    head_cols = pl.ds(pl.multiple_of(group * DH, DH), DH)
    own_k, own_v = k.at[:, head_cols], v.at[:, head_cols]
    wide = hid.shape[1] // G
    piece = wide // Z
    mine = at(p.slot, TOK)
    members = Y // KVG

    def strip(slot):
        return hid.at[:, pl.ds(pl.multiple_of(slot * wide, 128), wide)]

    moves = [
        (q, qg.at[mine]),
        (do, dog.at[mine]),
        (own_k, kg.at[at(place(0), TOK)]),
        (own_v, vg.at[at(place(0), TOK)]),
        (strip(p.slot), hg.at[mine]),
        (kw, tw.at[0]),
        (vw, tw.at[1]),
    ]
    everyone = plane_peers(p) + column_peers(p) + row_peers(p)
    greet(everyone)
    loads = [pltpu.make_async_copy(s, d, local.at[i]) for i, (s, d) in enumerate(moves)]
    for load in loads[5:] + loads[:5]:
        load.start()
    pg[p.slot] = jnp.broadcast_to(pos[...], (8, TOK))
    for i in range(2):
        loads[5 + i].wait()
        wsum[i] = jnp.broadcast_to(sum_squares(tw.at[i]), wsum.shape[1:])
    meet(everyone)
    copies = Copies(send, recv)
    small = [copies(pg.at[p.slot], pg.at[p.slot], peer) for peer in plane_peers(p)]
    kr = column_ring(copies, p, own_k, kg)
    vr = column_ring(copies, p, own_v, vg)
    qr = plane_direct(copies, p, q, whole(qg, TOK), TOK)
    dr = plane_direct(copies, p, do, whole(dog, TOK), TOK)
    for ring in (kr, vr, qr, dr):
        next(ring)
    for ring in (kr, vr):
        next(ring)
    for copy in small:
        copy.wait_recv()
    build_bias(owners, pg, bias, p)
    for ring in (kr, vr, qr):
        next(ring)
    for ring in (kr, vr, dr, kr, vr, qr, dr):
        next(ring, None)
    run(qr, dr)
    hs = []
    for s, f in ((2, False), (2, True), (1, False), (3, False), (1, True), (3, True), (0, True)):
        to = p.xslot(s, f)
        hs.append(copies(strip(to), hg.at[mine], p.in_plane(to)))
    for load in loads[:5]:
        load.wait()
    kt[...] = kg[...].T
    peers = plane_peers(p)
    mine_stats = shared.at[p.slot]

    def share(t):
        block = shared.at[p.slot, :, tile_of(t)]
        return [
            pltpu.make_async_remote_copy(
                src_ref=block,
                dst_ref=block,
                send_sem=share_send.at[n, t],
                recv_sem=share_recv.at[n, t],
                device_id=peer,
                device_id_type=MESH,
            )
            for n, peer in enumerate(peers)
        ]

    def stats_step(t, carry):
        tile_stats(qg, dog, kg, vg, bias, masses, dps, tops, mine_stats, t)
        for copy in share(t):
            copy.start()
        return carry

    tiles = qg.shape[0] // TILE
    lax.fori_loop(0, tiles, stats_step, 0)

    def ready(t):
        for copy in share(t):
            copy.wait_recv()
        merge_stats(shared, tops, merged, t)

    def scatter(chunk):
        count = Z // CHUNKS
        near = [s for s in FARTHEST if place(s) // count == chunk]
        return [
            [
                copies(src.at[at(place(s), TOK)], gz.at[i, p.z], p.in_column(p.zslot(s)))
                for s in near
            ]
            for i, src in enumerate((dk, dv))
        ]

    chunks = []
    for chunk in range(CHUNKS):
        chunk_grads(
            qg, dog, kt, masses, dps, merged, probs, slopes, acc, dqt, dq, dk, dv, chunk,
            ready if chunk == 0 else lambda t: None,
        )
        chunks.append(scatter(chunk))
    own_g = [
        pltpu.make_async_copy(src.at[at(place(0), TOK)], gz.at[i, p.z], local.at[7 + i])
        for i, src in enumerate((dk, dv))
    ]
    for load in own_g:
        load.start()

    def stream(i, raw):
        made = [copy for parts in chunks for copy in parts[i]]
        own_g[i].wait()
        for copy in made:
            copy.wait_recv()
        gy[i, p.y] = rounded_sum(gz, i, Z)
        made = [copies(gy.at[i, p.y], gy.at[i, p.y], peer) for peer in row_peers(p)]
        yield
        for copy in made:
            copy.wait_recv()
        for g in range(KVG):
            total = gy[i, g * members].astype(F32)
            for n in range(1, members):
                total = total + gy[i, g * members + n].astype(F32)
            grads[i, mine, g * DH : (g + 1) * DH] = total.astype(BF16)
        ring = plane_direct(copies, p, grads.at[i, mine], whole(grads.at[i], TOK), TOK)
        for _ in ring:
            yield
        product = jnp.dot(hgt[...], grads[i], preferred_element_type=F32)
        part[i] = product.astype(BF16)
        rz[i, p.z] = part[i, at(p.z, piece), :]
        made = [
            copies(part.at[i, at(p.zslot(s), piece)], rz.at[i, p.z], p.in_column(p.zslot(s)))
            for s in FARTHEST
        ]
        yield
        for copy in made:
            copy.wait_recv()
        own = at(p.z, piece)
        block[i, own, :] = rounded_sum(rz, i, Z)
        made = [
            copies(block.at[i, own], block.at[i, own], p.in_column(p.zslot(s)))
            for s in FARTHEST
        ]
        yield
        for copy in made:
            copy.wait_recv()
        ring = plane_ring(copies, p, block.at[i], whole(raw, wide), wide)
        next(ring)
        puts = [
            pltpu.make_async_copy(block.at[i], raw.at[at(p.slot, wide)], local.at[9 + i]),
            pltpu.make_async_copy(tot.at[i], sums.at[i, p.slot], local.at[11 + i]),
        ]
        puts[0].start()
        square = sum_squares(block.at[i])
        row = lax.broadcasted_iota(jnp.int32, (8, square.shape[1]), 0)
        ysum[i, p.y] = jnp.where(row == 0, square, wsum[i])
        made = [copies(ysum.at[i, p.y], ysum.at[i, p.y], peer) for peer in row_peers(p)]
        yield
        next(ring)
        for copy in made:
            copy.wait_recv()
        total = ysum[i, 0]
        for n in range(1, Y):
            total = total + ysum[i, n]
        tot[i] = total
        puts[1].start()
        made = [copies(tot.at[i], sums.at[i, p.slot], peer) for peer in plane_peers(p)]
        yield
        next(ring)
        yield
        for _ in ring:
            pass
        for copy in made:
            copy.wait_recv()
        for put in puts:
            put.wait()

    partner = p.in_plane(p.xslot(0, True))
    given = [copies(dq.at[at(x * C + 1 - p.c, TOK)], pq.at[x], partner) for x in range(X)]
    for copy in hs:
        copy.wait_recv()
    hgt[...] = hg[...].T
    streams = [stream(0, raw_k), stream(1, raw_v)]
    for one in streams:
        next(one)
    for x in range(X):
        given[x].wait_recv()
        cq[x] = (dq[at(x * C + p.c, TOK), :].astype(F32) + pq[x].astype(F32)).astype(BF16)
    qs = []
    for s in (2, 1, 3):
        to = lax.rem(p.x + s, X)
        qs.append(copies(cq.at[to], dq_slots.at[p.x], p.in_plane(to * C + p.c)))
    put_q = pltpu.make_async_copy(cq.at[p.x], dq_slots.at[p.x], local.at[13])
    put_q.start()
    run(*streams)
    for copy in qs:
        copy.wait_recv()
    put_q.wait()
    copies.wait_sends()
    for t in range(tiles):
        for copy in share(t):
            copy.wait_send()


def shape(dims, kind=BF16):
    return jax.ShapeDtypeStruct(dims, kind)


def dma(n):
    return pltpu.SemaphoreType.DMA((n,))


def local(
    queries, keys, values, out_grad, hidden, key_weight, value_weight, stretch_owner, positions
):
    width = queries.shape[1]
    model = hidden.shape[1]
    piece = model // G
    columns = KVG * DH
    dq_slots, raw_k, raw_v, sums = pl.pallas_call(
        kernel,
        out_shape=(
            pltpu.VMEM((X, TOK, width), BF16),
            pltpu.VMEM((model, columns), BF16),
            pltpu.VMEM((model, columns), BF16),
            pltpu.VMEM((2, G, 8, columns), F32),
        ),
        in_specs=[SMEM] + [ANY] * 4 + [VMEM] + [ANY] * 3,
        out_specs=(ANY,) * 4,
        scratch_shapes=[
            pltpu.VMEM((ROWS, width), BF16),
            pltpu.VMEM((ROWS, width), BF16),
            pltpu.VMEM((Z * TOK, DH), BF16),
            pltpu.VMEM((Z * TOK, DH), BF16),
            pltpu.VMEM((G, 8, TOK), jnp.int32),
            pltpu.VMEM((Z * TOK, ROWS), F32),
            pltpu.VMEM((G, 2 * HEADS, ROWS), F32),
            pltpu.VMEM((2 * HEADS, ROWS), F32),
            pltpu.VMEM((DH, Z * TOK), BF16),
            pltpu.VMEM((Z * TOK, HEADS * ROWS), BF16),
            pltpu.VMEM((Z * TOK, HEADS * ROWS), F32),
            pltpu.VMEM((8, ROWS), F32),
            pltpu.VMEM((Z * TOK // CHUNKS, HEADS * TILE), BF16),
            pltpu.VMEM((Z * TOK // CHUNKS, HEADS * TILE), BF16),
            pltpu.VMEM((Z * TOK // CHUNKS, 2 * DH), F32),
            pltpu.VMEM((ROWS // TILE, DH, HEADS * TILE), F32),
            pltpu.VMEM((ROWS, width), BF16),
            pltpu.VMEM((Z * TOK, DH), BF16),
            pltpu.VMEM((Z * TOK, DH), BF16),
            pltpu.VMEM((ROWS, piece), BF16),
            pltpu.VMEM((piece, ROWS), BF16),
            pltpu.VMEM((X, TOK, width), BF16),
            pltpu.VMEM((X, TOK, width), BF16),
            pltpu.VMEM((2, Z, TOK, DH), BF16),
            pltpu.VMEM((2, Y, TOK, DH), BF16),
            pltpu.VMEM((2, ROWS, columns), BF16),
            pltpu.VMEM((2, piece, columns), BF16),
            pltpu.VMEM((2, Z, piece // Z, columns), BF16),
            pltpu.VMEM((2, Y, 8, columns), F32),
            pltpu.VMEM((2, 8, columns), F32),
            pltpu.VMEM((2, model, columns), BF16),
            pltpu.VMEM((2, piece, columns), BF16),
            pltpu.VMEM((2, 8, columns), F32),
            dma(180),
            dma(180),
            pltpu.SemaphoreType.DMA((G - 1, ROWS // TILE)),
            pltpu.SemaphoreType.DMA((G - 1, ROWS // TILE)),
            dma(14),
        ],
        compiler_params=pltpu.CompilerParams(
            collective_id=0, has_side_effects=True, vmem_limit_bytes=VMEM_BYTES
        ),
    )(
        stretch_owner, queries, out_grad, keys, values, positions.reshape(1, TOK),
        hidden, key_weight, value_weight,
    )
    query_grad = jnp.sum(dq_slots.astype(F32), axis=0).astype(BF16)
    tokens = TOK * PAIRS

    def clipped(i, raw):
        grad_norm = jnp.sqrt(jnp.sum(sums[i, :, 0], axis=0) + EPSILON)
        weight_norm = jnp.sqrt(sums[i, 0, 1] + EPSILON)
        factor = jnp.minimum(1.0, CLIP_RATE * tokens * weight_norm / grad_norm)
        return raw.astype(F32) * factor[None, :]

    return (query_grad, clipped(0, raw_k), clipped(1, raw_v))


def solution(mesh):
    return jax.shard_map(
        local,
        mesh=mesh,
        in_specs=(
            P("ctx", "fsdp"),
            P("ctx", None),
            P("ctx", None),
            P("ctx", "fsdp"),
            P("ctx", "fsdp"),
            P("fsdp", None),
            P("fsdp", None),
            P(),
            P("ctx"),
        ),
        out_specs=(P("ctx", "fsdp"), P("fsdp", None), P("fsdp", None)),
        check_vma=False,
    )
```

```python
import functools
import math

import jax
import jax.numpy as jnp
from jax import lax
from jax.experimental import pallas as pl
from jax.experimental.pallas import tpu as pltpu
from jax.sharding import PartitionSpec as P

DH = 128
HPG = 8
KVG = 2
TOK = 128
HALF = TOK // 2
Z = 8
X = 4
C = 2
Y = 4
G = X * C
PAIRS = Z * X * C
HEADS = 4
ROWS = G * TOK
CLIP_RATE = 0.02
TILE = 256
VMEM_BYTES = 55 * 1024 * 1024
CHUNKS = 4
SENDS = 24
RECVS = 56
ORDER = (3, 5, 4, 2, 6, 1, 7, 0)
EPSILON = 1e-06
NEGATIVE = -1e30
SCALE = 1.0 / math.sqrt(DH)
SCALE2 = SCALE * math.log2(math.e)
MESH = pl.DeviceIdType.MESH
ANY = pl.BlockSpec(memory_space=pl.ANY)
VMEM = pl.BlockSpec(memory_space=pltpu.VMEM)
HBM = pl.BlockSpec(memory_space=pltpu.HBM)
SMEM = pl.BlockSpec(memory_space=pltpu.SMEM)
LAST = (((1,), (1,)), ((), ()))
FIRST = (((0,), (0,)), ((), ()))
BF16 = jnp.bfloat16
F32 = jnp.float32


class Place:
    def __init__(self):
        me = lax.axis_index("ctx")
        self.me = me
        self.y = lax.axis_index("fsdp")
        self.z = lax.div(me, G)
        self.slot = lax.rem(me, G)
        self.x = lax.div(self.slot, C)
        self.c = lax.rem(self.slot, C)

    def xslot(self, step, flip=False):
        x = lax.rem(self.x + step + X, X)
        return x * C + ((1 - self.c) if flip else self.c)

    def in_plane(self, slot):
        return {"ctx": self.z * G + slot}

    def zslot(self, step):
        return lax.rem(self.z + step + Z, Z)

    def in_column(self, z):
        return {"ctx": z * G + self.slot}

    def yslot(self, step):
        return lax.rem(self.y + step, Y)


class Copies:
    def __init__(self, send, recv):
        self.send, self.recv, self.groups, self.slots = send, recv, [], 0

    def group(self, region):
        self.groups.append(region)
        return len(self.groups) - 1

    def slot(self):
        self.slots += 1
        return self.slots - 1

    def start(self, src, dst, device, group, slot):
        copy = pltpu.make_async_remote_copy(
            src_ref=src,
            dst_ref=dst,
            send_sem=self.send.at[group],
            recv_sem=self.recv.at[slot],
            device_id=device,
            device_id_type=MESH,
        )
        copy.start()
        return copy

    def wait_sends(self):
        for i, region in enumerate(self.groups):
            take(region, self.send.at[i])


def take(region, sem):
    pltpu.make_async_copy(region, region, sem).wait()


class Batch:
    def __init__(self, copies, region, group=None):
        self.copies, self.region = copies, region
        self.group = copies.group(region) if group is None else group
        self.slot = copies.slot()

    def add(self, src, dst, device):
        self.copies.start(src, dst, device, self.group, self.slot)

    def wait_recv(self):
        take(self.region, self.copies.recv.at[self.slot])


class Chain:
    def __init__(self, copies, region):
        self.copies, self.group = copies, copies.group(region)

    def __call__(self, src, dst, device):
        return self.copies.start(src, dst, device, self.group, self.copies.slot())


def greet(devices):
    for device in devices:
        pl.semaphore_signal(
            pltpu.get_barrier_semaphore(), inc=1, device_id=device, device_id_type=MESH
        )


def meet(devices):
    pl.semaphore_wait(pltpu.get_barrier_semaphore(), len(devices))


def at(slot, rows, offset=0, count=None):
    return pl.ds(pl.multiple_of(slot * rows + offset, 16), rows if count is None else count)


def plane_ring(copies, p, src, where, rows):
    half = rows // 2
    right, left = p.xslot(1), p.xslot(-1)
    partner = p.in_plane(p.xslot(0, True))
    chain = Chain(copies, where(0, 0, (G - 1) * rows))
    passed = Batch(copies, where(0, 0, X * rows), chain.group)

    def hand(slot):
        block = where(slot, 0, rows)
        passed.add(block, block, partner)

    mine = where(p.slot, 0, rows)
    a = chain(src, mine, p.in_plane(right))
    b = chain(src, mine, p.in_plane(left))
    passed.add(src, mine, partner)
    yield
    a.wait_recv()
    first = where(left, 0, half)
    f = chain(first, first, p.in_plane(right))
    hand(left)
    b.wait_recv()
    second = where(right, half, half)
    g = chain(second, second, p.in_plane(left))
    hand(right)
    yield
    f.wait_recv()
    g.wait_recv()
    hand(p.xslot(2))
    yield
    passed.wait_recv()


def plane_direct(copies, p, src, where, rows):
    partner = p.in_plane(p.xslot(0, True))
    chain = Chain(copies, where(0, 0, (G - 1) * rows))
    passed = Batch(copies, where(0, 0, X * rows), chain.group)

    def hand(slot):
        block = where(slot, 0, rows)
        passed.add(block, block, partner)

    mine = where(p.slot, 0, rows)
    c, a, b = [chain(src, mine, p.in_plane(p.xslot(s))) for s in (2, 1, -1)]
    passed.add(src, mine, partner)
    yield
    a.wait_recv()
    hand(p.xslot(-1))
    b.wait_recv()
    hand(p.xslot(1))
    yield
    c.wait_recv()
    hand(p.xslot(2))
    yield
    passed.wait_recv()


def whole(ref, rows):
    return lambda slot, offset, count: ref.at[at(slot, rows, offset, count)]


def column_ring(copies, p, src, ref):
    def block(distance):
        return ref.at[at(place(distance), TOK)]

    up, down = p.in_column(p.zslot(1)), p.in_column(p.zslot(-1))
    chain = Chain(copies, ref.at[pl.ds(0, (Z - 1) * TOK)])
    u = chain(src, block(-1), up)
    d = chain(src, block(1), down)
    for step in range(1, Z // 2 + 1):
        yield
        u.wait_recv()
        if step < Z // 2:
            u = chain(block(-step), block(-step - 1), up)
        if step < Z // 2:
            d.wait_recv()
            if step < Z // 2 - 1:
                d = chain(block(step), block(step + 1), down)


def run(*rings):
    rings = list(rings)
    while rings:
        rings = [ring for ring in rings if next(ring, True) is None]


def plane_peers(p):
    return [p.in_plane(p.xslot(s, f)) for s in range(X) for f in (False, True) if s or f]


def column_peers(p):
    return [p.in_column(p.zslot(s)) for s in range(1, Z)]


def row_peers(p):
    return [{"fsdp": p.yslot(s)} for s in range(1, Y)]


def sum_squares(ref, chunk=64):
    width = ref.shape[1]

    def step(i, acc):
        block = ref[pl.ds(pl.multiple_of(i * chunk, chunk), chunk), :].astype(F32)
        return acc + jnp.sum((block * block).reshape(chunk // 8, 8, width), axis=0)

    acc = lax.fori_loop(0, ref.shape[0] // chunk, step, jnp.zeros((8, width), F32))
    return jnp.sum(acc, axis=0, keepdims=True)


def place(distance):
    return ORDER.index(distance % Z)


def sum_squares(ref, chunk=64):
    width = ref.shape[1]

    def step(i, acc):
        block = ref[pl.ds(pl.multiple_of(i * chunk, chunk), chunk), :].astype(F32)
        return acc + jnp.sum((block * block).reshape(chunk // 8, 8, width), axis=0)

    acc = lax.fori_loop(0, ref.shape[0] // chunk, step, jnp.zeros((8, width), F32))
    return jnp.sum(acc, axis=0, keepdims=True)


def build_bias(owners, pos, bias, p):
    lane = lax.broadcasted_iota(jnp.int32, (1, TOK), 1)
    low = lane < HALF
    row = lax.broadcasted_iota(jnp.int32, (HALF, TOK), 0)

    def step(slot, carry):
        owner = owners[p.z * G + slot]
        where = lane + jnp.where(low, owner * HALF, (2 * PAIRS - 1 - owner) * HALF - HALF)
        floor = where - pos[slot, 0:1, :]
        cols = pl.ds(pl.multiple_of(slot * TOK, TOK), TOK)
        for distance in range(Z):
            owner = owners[p.zslot(distance) * G + p.slot]
            for h, stretch in enumerate((owner, 2 * PAIRS - 1 - owner)):
                key = row + stretch * HALF
                seen = (key <= where) & (key >= floor)
                rows = pl.ds(place(distance) * TOK + h * HALF, HALF)
                bias[rows, cols] = jnp.where(seen, 0.0, NEGATIVE)
        return carry

    lax.fori_loop(0, G, step, 0)


def tile_of(t):
    return pl.ds(pl.multiple_of(t * TILE, TILE), TILE)


def head_of(t, h):
    return pl.ds(pl.multiple_of((t * HEADS + h) * TILE, TILE), TILE)


def tile_stats(qg, dog, kg, vg, bias, masses, dps, tops, out, t):
    tile = tile_of(t)
    for h in range(HEADS):
        cols = pl.ds(h * DH, DH)
        raw = lax.dot_general(kg[...], qg[tile, cols], LAST, preferred_element_type=F32)
        raw = raw + bias[:, tile]
        top = jnp.max(raw, axis=0, keepdims=True)
        mass = jnp.exp2((raw - top) * SCALE2)
        total = jnp.sum(mass, axis=0, keepdims=True)
        masses[:, head_of(t, h)] = mass.astype(BF16)
        dp = lax.dot_general(vg[...], dog[tile, cols], LAST, preferred_element_type=F32)
        dps[:, head_of(t, h)] = dp
        dsum = jnp.sum(mass * dp, axis=0, keepdims=True)
        tops[h : h + 1, tile] = top * SCALE2
        out[h : h + 1, tile] = top * SCALE2 + jnp.log2(total)
        out[HEADS + h : HEADS + h + 1, tile] = dsum / total


def merge_stats(shared, tops, merged, t):
    tile = tile_of(t)
    for h in range(HEADS):
        parts = shared[:, h, tile]
        top = jnp.max(parts, axis=0, keepdims=True)
        weight = jnp.exp2(parts - top)
        total = jnp.sum(weight, axis=0, keepdims=True)
        merged[h : h + 1, tile] = jnp.exp2(tops[h : h + 1, tile] - (top + jnp.log2(total)))
        dsum = jnp.sum(weight * shared[:, HEADS + h, tile], axis=0, keepdims=True)
        merged[HEADS + h : HEADS + h + 1, tile] = dsum / total


def chunk_grads(
    qg, dog, kt, masses, dps, merged, probs, slopes, acc, dqt, dq, dk, dv, chunk, ready
):
    count = masses.shape[0] // CHUNKS
    rows = pl.ds(chunk * count, count)
    acc[...] = jnp.zeros_like(acc)

    def step(t, carry):
        ready(t)
        tile = tile_of(t)
        for h in range(HEADS):
            cols = pl.ds(h * DH, DH)
            wide = pl.ds(h * TILE, TILE)
            prob = masses[rows, head_of(t, h)].astype(F32) * merged[h : h + 1, tile]
            slope = prob * (dps[rows, head_of(t, h)] - merged[HEADS + h : HEADS + h + 1, tile])
            probs[:, wide] = prob.astype(BF16)
            slopes[:, wide] = slope.astype(BF16)
            part = jnp.dot(kt[:, rows], slopes[:, wide], preferred_element_type=F32)
            if chunk > 0:
                part = part + dqt[t, :, wide]
            if chunk < CHUNKS - 1:
                dqt[t, :, wide] = part
            else:
                dq[tile, cols] = (part * SCALE).T.astype(BF16)
        tall = lambda ref: jnp.concatenate(
            [ref[tile, pl.ds(h * DH, DH)] for h in range(HEADS)], axis=0
        )
        acc[:, :DH] += jnp.dot(slopes[...], tall(qg), preferred_element_type=F32)
        acc[:, DH:] += jnp.dot(probs[...], tall(dog), preferred_element_type=F32)
        return carry

    lax.fori_loop(0, qg.shape[0] // TILE, step, 0)
    dk[rows, :] = (acc[:, :DH] * SCALE).astype(BF16)
    dv[rows, :] = acc[:, DH:].astype(BF16)


FARTHEST = (4, 3, 5, 2, 6, 1, 7)


def rounded_sum(ref, i, count):
    total = ref[i, 0].astype(F32)
    for n in range(1, count):
        total = total + ref[i, n].astype(F32)
    return total.astype(BF16)


def kernel(
    owners, q, do, k, v, pos, hid, kw, vw, dq_slots, raw_k, raw_v, sums,
    qg, dog, kg, vg, pg, bias, shared, merged, kt, masses, dps, tops, probs, slopes, acc, dqt, dq, dk, dv,
    hg, hgt, pq, cq, gz, gy, grads, part, rz, ysum, wsum, tw, block, tot,
    send, recv, share_send, share_recv, local,
):
    p = Place()
    group = lax.div(p.y * HEADS, HPG)
    head_cols = pl.ds(pl.multiple_of(group * DH, DH), DH)
    own_k, own_v = k.at[:, head_cols], v.at[:, head_cols]
    wide = hid.shape[1] // G
    piece = wide // Z
    mine = at(p.slot, TOK)
    members = Y // KVG

    def strip(slot):
        return hid.at[:, pl.ds(pl.multiple_of(slot * wide, 128), wide)]

    moves = [
        (q, qg.at[mine]),
        (do, dog.at[mine]),
        (own_k, kg.at[at(place(0), TOK)]),
        (own_v, vg.at[at(place(0), TOK)]),
        (strip(p.slot), hg.at[mine]),
        (kw, tw.at[0]),
        (vw, tw.at[1]),
    ]
    everyone = plane_peers(p) + column_peers(p) + row_peers(p)
    greet(everyone)
    loads = [pltpu.make_async_copy(s, d, local.at[i]) for i, (s, d) in enumerate(moves)]
    for load in loads[5:] + loads[:5]:
        load.start()
    pg[p.slot] = jnp.broadcast_to(pos[...], (8, TOK))
    for i in range(2):
        loads[5 + i].wait()
        wsum[i] = jnp.broadcast_to(sum_squares(tw.at[i]), wsum.shape[1:])
    meet(everyone)
    copies = Copies(send, recv)
    small = Batch(copies, pg.at[pl.ds(0, G - 1)])
    for peer in plane_peers(p):
        small.add(pg.at[p.slot], pg.at[p.slot], peer)
    kr = column_ring(copies, p, own_k, kg)
    vr = column_ring(copies, p, own_v, vg)
    qr = plane_direct(copies, p, q, whole(qg, TOK), TOK)
    dr = plane_direct(copies, p, do, whole(dog, TOK), TOK)
    for ring in (kr, vr, qr, dr):
        next(ring)
    for ring in (kr, vr):
        next(ring)
    small.wait_recv()
    build_bias(owners, pg, bias, p)
    for ring in (kr, vr, qr):
        next(ring)
    for ring in (kr, vr, dr, kr, vr, qr, dr):
        next(ring, None)
    run(qr, dr)
    hs = Batch(copies, hg.at[pl.ds(0, (G - 1) * TOK)])
    for s, f in ((2, False), (2, True), (1, False), (3, False), (1, True), (3, True), (0, True)):
        to = p.xslot(s, f)
        hs.add(strip(to), hg.at[mine], p.in_plane(to))
    for load in loads[:5]:
        load.wait()
    kt[...] = kg[...].T
    peers = plane_peers(p)
    mine_stats = shared.at[p.slot]

    def share(t):
        block = shared.at[p.slot, :, tile_of(t)]
        return [
            pltpu.make_async_remote_copy(
                src_ref=block,
                dst_ref=block,
                send_sem=share_send.at[0],
                recv_sem=share_recv.at[t],
                device_id=peer,
                device_id_type=MESH,
            )
            for peer in peers
        ]

    def stats_step(t, carry):
        tile_stats(qg, dog, kg, vg, bias, masses, dps, tops, mine_stats, t)
        for copy in share(t):
            copy.start()
        return carry

    tiles = qg.shape[0] // TILE
    lax.fori_loop(0, tiles, stats_step, 0)

    def ready(t):
        take(shared.at[pl.ds(0, G - 1), :, tile_of(t)], share_recv.at[t])
        merge_stats(shared, tops, merged, t)

    scattered = [Batch(copies, gz.at[i, pl.ds(0, Z - 1)]) for i in range(2)]

    def scatter(chunk):
        count = Z // CHUNKS
        for i, src in enumerate((dk, dv)):
            for s in FARTHEST:
                if place(s) // count == chunk:
                    scattered[i].add(
                        src.at[at(place(s), TOK)], gz.at[i, p.z], p.in_column(p.zslot(s))
                    )

    for chunk in range(CHUNKS):
        chunk_grads(
            qg, dog, kt, masses, dps, merged, probs, slopes, acc, dqt, dq, dk, dv, chunk,
            ready if chunk == 0 else lambda t: None,
        )
        scatter(chunk)
    own_g = [
        pltpu.make_async_copy(src.at[at(place(0), TOK)], gz.at[i, p.z], local.at[7 + i])
        for i, src in enumerate((dk, dv))
    ]
    for load in own_g:
        load.start()

    def stream(i, raw):
        own_g[i].wait()
        scattered[i].wait_recv()
        gy[i, p.y] = rounded_sum(gz, i, Z)
        made = Batch(copies, gy.at[i, pl.ds(0, Y - 1)])
        for peer in row_peers(p):
            made.add(gy.at[i, p.y], gy.at[i, p.y], peer)
        yield
        made.wait_recv()
        for g in range(KVG):
            total = gy[i, g * members].astype(F32)
            for n in range(1, members):
                total = total + gy[i, g * members + n].astype(F32)
            grads[i, mine, g * DH : (g + 1) * DH] = total.astype(BF16)
        ring = plane_direct(copies, p, grads.at[i, mine], whole(grads.at[i], TOK), TOK)
        for _ in ring:
            yield
        product = jnp.dot(hgt[...], grads[i], preferred_element_type=F32)
        part[i] = product.astype(BF16)
        rz[i, p.z] = part[i, at(p.z, piece), :]
        made = Batch(copies, rz.at[i, pl.ds(0, Z - 1)])
        for s in FARTHEST:
            made.add(part.at[i, at(p.zslot(s), piece)], rz.at[i, p.z], p.in_column(p.zslot(s)))
        yield
        made.wait_recv()
        own = at(p.z, piece)
        block[i, own, :] = rounded_sum(rz, i, Z)
        made = Batch(copies, block.at[i, pl.ds(0, (Z - 1) * piece)])
        for s in FARTHEST:
            made.add(block.at[i, own], block.at[i, own], p.in_column(p.zslot(s)))
        yield
        made.wait_recv()
        ring = plane_ring(copies, p, block.at[i], whole(raw, wide), wide)
        next(ring)
        puts = [
            pltpu.make_async_copy(block.at[i], raw.at[at(p.slot, wide)], local.at[9 + i]),
            pltpu.make_async_copy(tot.at[i], sums.at[i, p.slot], local.at[11 + i]),
        ]
        puts[0].start()
        square = sum_squares(block.at[i])
        row = lax.broadcasted_iota(jnp.int32, (8, square.shape[1]), 0)
        ysum[i, p.y] = jnp.where(row == 0, square, wsum[i])
        made = Batch(copies, ysum.at[i, pl.ds(0, Y - 1)])
        for peer in row_peers(p):
            made.add(ysum.at[i, p.y], ysum.at[i, p.y], peer)
        yield
        next(ring)
        made.wait_recv()
        total = ysum[i, 0]
        for n in range(1, Y):
            total = total + ysum[i, n]
        tot[i] = total
        puts[1].start()
        made = Batch(copies, sums.at[i, pl.ds(0, G - 1)])
        for peer in plane_peers(p):
            made.add(tot.at[i], sums.at[i, p.slot], peer)
        yield
        next(ring)
        yield
        for _ in ring:
            pass
        made.wait_recv()
        for put in puts:
            put.wait()

    partner = p.in_plane(p.xslot(0, True))
    given = Batch(copies, pq)
    for x in range(X):
        given.add(dq.at[at(x * C + 1 - p.c, TOK)], pq.at[x], partner)
    hs.wait_recv()
    hgt[...] = hg[...].T
    streams = [stream(0, raw_k), stream(1, raw_v)]
    for one in streams:
        next(one)
    given.wait_recv()
    for x in range(X):
        cq[x] = (dq[at(x * C + p.c, TOK), :].astype(F32) + pq[x].astype(F32)).astype(BF16)
    put_q = pltpu.make_async_copy(cq.at[p.x], dq_slots.at[p.x], local.at[13])
    put_q.start()
    for _ in range(3):
        for one in streams:
            next(one)
    qs = Batch(copies, dq_slots.at[pl.ds(0, X - 1)])
    for s in (2, 1, 3):
        to = lax.rem(p.x + s, X)
        qs.add(cq.at[to], dq_slots.at[p.x], p.in_plane(to * C + p.c))
    run(*streams)
    qs.wait_recv()
    put_q.wait()
    copies.wait_sends()
    take(shared.at[pl.ds(0, G - 1)], share_send.at[0])


def shape(dims, kind=BF16):
    return jax.ShapeDtypeStruct(dims, kind)


def dma(n):
    return pltpu.SemaphoreType.DMA((n,))


def local(
    queries, keys, values, out_grad, hidden, key_weight, value_weight, stretch_owner, positions
):
    width = queries.shape[1]
    model = hidden.shape[1]
    piece = model // G
    columns = KVG * DH
    dq_slots, raw_k, raw_v, sums = pl.pallas_call(
        kernel,
        out_shape=(
            pltpu.VMEM((X, TOK, width), BF16),
            pltpu.VMEM((model, columns), BF16),
            pltpu.VMEM((model, columns), BF16),
            pltpu.VMEM((2, G, 8, columns), F32),
        ),
        in_specs=[SMEM] + [ANY] * 4 + [VMEM] + [ANY] * 3,
        out_specs=(ANY,) * 4,
        scratch_shapes=[
            pltpu.VMEM((ROWS, width), BF16),
            pltpu.VMEM((ROWS, width), BF16),
            pltpu.VMEM((Z * TOK, DH), BF16),
            pltpu.VMEM((Z * TOK, DH), BF16),
            pltpu.VMEM((G, 8, TOK), jnp.int32),
            pltpu.VMEM((Z * TOK, ROWS), F32),
            pltpu.VMEM((G, 2 * HEADS, ROWS), F32),
            pltpu.VMEM((2 * HEADS, ROWS), F32),
            pltpu.VMEM((DH, Z * TOK), BF16),
            pltpu.VMEM((Z * TOK, HEADS * ROWS), BF16),
            pltpu.VMEM((Z * TOK, HEADS * ROWS), F32),
            pltpu.VMEM((8, ROWS), F32),
            pltpu.VMEM((Z * TOK // CHUNKS, HEADS * TILE), BF16),
            pltpu.VMEM((Z * TOK // CHUNKS, HEADS * TILE), BF16),
            pltpu.VMEM((Z * TOK // CHUNKS, 2 * DH), F32),
            pltpu.VMEM((ROWS // TILE, DH, HEADS * TILE), F32),
            pltpu.VMEM((ROWS, width), BF16),
            pltpu.VMEM((Z * TOK, DH), BF16),
            pltpu.VMEM((Z * TOK, DH), BF16),
            pltpu.VMEM((ROWS, piece), BF16),
            pltpu.VMEM((piece, ROWS), BF16),
            pltpu.VMEM((X, TOK, width), BF16),
            pltpu.VMEM((X, TOK, width), BF16),
            pltpu.VMEM((2, Z, TOK, DH), BF16),
            pltpu.VMEM((2, Y, TOK, DH), BF16),
            pltpu.VMEM((2, ROWS, columns), BF16),
            pltpu.VMEM((2, piece, columns), BF16),
            pltpu.VMEM((2, Z, piece // Z, columns), BF16),
            pltpu.VMEM((2, Y, 8, columns), F32),
            pltpu.VMEM((2, 8, columns), F32),
            pltpu.VMEM((2, model, columns), BF16),
            pltpu.VMEM((2, piece, columns), BF16),
            pltpu.VMEM((2, 8, columns), F32),
            dma(SENDS),
            dma(RECVS),
            dma(1),
            dma(ROWS // TILE),
            dma(14),
        ],
        compiler_params=pltpu.CompilerParams(
            collective_id=0, has_side_effects=True, vmem_limit_bytes=VMEM_BYTES
        ),
    )(
        stretch_owner, queries, out_grad, keys, values, positions.reshape(1, TOK),
        hidden, key_weight, value_weight,
    )
    query_grad = jnp.sum(dq_slots.astype(F32), axis=0).astype(BF16)
    tokens = TOK * PAIRS

    def clipped(i, raw):
        grad_norm = jnp.sqrt(jnp.sum(sums[i, :, 0], axis=0) + EPSILON)
        weight_norm = jnp.sqrt(sums[i, 0, 1] + EPSILON)
        factor = jnp.minimum(1.0, CLIP_RATE * tokens * weight_norm / grad_norm)
        return raw.astype(F32) * factor[None, :]

    return (query_grad, clipped(0, raw_k), clipped(1, raw_v))


def solution(mesh):
    return jax.shard_map(
        local,
        mesh=mesh,
        in_specs=(
            P("ctx", "fsdp"),
            P("ctx", None),
            P("ctx", None),
            P("ctx", "fsdp"),
            P("ctx", "fsdp"),
            P("fsdp", None),
            P("fsdp", None),
            P(),
            P("ctx"),
        ),
        out_specs=(P("ctx", "fsdp"), P("fsdp", None), P("fsdp", None)),
        check_vma=False,
    )
```

```python
import functools
import math

import jax
import jax.numpy as jnp
from jax import lax
from jax.experimental import pallas as pl
from jax.experimental.pallas import tpu as pltpu
from jax.sharding import PartitionSpec as P

DH = 128
HPG = 8
KVG = 2
TOK = 128
HALF = TOK // 2
Z = 8
X = 4
C = 2
Y = 4
G = X * C
PAIRS = Z * X * C
HEADS = 4
ROWS = G * TOK
CLIP_RATE = 0.02
TILE = 256
VMEM_BYTES = 55 * 1024 * 1024
CHUNKS = 4
SENDS = 24
RECVS = 56
ORDER = (3, 5, 4, 2, 6, 1, 7, 0)
EPSILON = 1e-06
NEGATIVE = -1e30
SCALE = 1.0 / math.sqrt(DH)
SCALE2 = SCALE * math.log2(math.e)
MESH = pl.DeviceIdType.MESH
ANY = pl.BlockSpec(memory_space=pl.ANY)
VMEM = pl.BlockSpec(memory_space=pltpu.VMEM)
HBM = pl.BlockSpec(memory_space=pltpu.HBM)
SMEM = pl.BlockSpec(memory_space=pltpu.SMEM)
LAST = (((1,), (1,)), ((), ()))
FIRST = (((0,), (0,)), ((), ()))
BF16 = jnp.bfloat16
F32 = jnp.float32


class Place:
    def __init__(self):
        me = lax.axis_index("ctx")
        self.me = me
        self.y = lax.axis_index("fsdp")
        self.z = lax.div(me, G)
        self.slot = lax.rem(me, G)
        self.x = lax.div(self.slot, C)
        self.c = lax.rem(self.slot, C)

    def xslot(self, step, flip=False):
        x = lax.rem(self.x + step + X, X)
        return x * C + ((1 - self.c) if flip else self.c)

    def in_plane(self, slot):
        return {"ctx": self.z * G + slot}

    def zslot(self, step):
        return lax.rem(self.z + step + Z, Z)

    def in_column(self, z):
        return {"ctx": z * G + self.slot}

    def yslot(self, step):
        return lax.rem(self.y + step, Y)


class Copies:
    def __init__(self, send, recv):
        self.send, self.recv, self.groups, self.slots = send, recv, [], 0

    def group(self, region):
        self.groups.append(region)
        return len(self.groups) - 1

    def slot(self):
        self.slots += 1
        return self.slots - 1

    def start(self, src, dst, device, group, slot):
        copy = pltpu.make_async_remote_copy(
            src_ref=src,
            dst_ref=dst,
            send_sem=self.send.at[group],
            recv_sem=self.recv.at[slot],
            device_id=device,
            device_id_type=MESH,
        )
        copy.start()
        return copy

    def wait_sends(self):
        for i, region in enumerate(self.groups):
            take(region, self.send.at[i])


def take(region, sem):
    pltpu.make_async_copy(region, region, sem).wait()


class Batch:
    def __init__(self, copies, region, group=None):
        self.copies, self.region = copies, region
        self.group = copies.group(region) if group is None else group
        self.slot = copies.slot()

    def add(self, src, dst, device):
        self.copies.start(src, dst, device, self.group, self.slot)

    def wait_recv(self):
        take(self.region, self.copies.recv.at[self.slot])


class Chain:
    def __init__(self, copies, region):
        self.copies, self.group = copies, copies.group(region)

    def __call__(self, src, dst, device):
        return self.copies.start(src, dst, device, self.group, self.copies.slot())


def greet(devices):
    for device in devices:
        pl.semaphore_signal(
            pltpu.get_barrier_semaphore(), inc=1, device_id=device, device_id_type=MESH
        )


def meet(devices):
    pl.semaphore_wait(pltpu.get_barrier_semaphore(), len(devices))


def at(slot, rows, offset=0, count=None):
    return pl.ds(pl.multiple_of(slot * rows + offset, 16), rows if count is None else count)


def plane_ring(copies, p, src, where, rows):
    half = rows // 2
    right, left = p.xslot(1), p.xslot(-1)
    partner = p.in_plane(p.xslot(0, True))
    chain = Chain(copies, where(0, 0, (G - 1) * rows))
    passed = Batch(copies, where(0, 0, X * rows), chain.group)

    def hand(slot):
        block = where(slot, 0, rows)
        passed.add(block, block, partner)

    mine = where(p.slot, 0, rows)
    a = chain(src, mine, p.in_plane(right))
    b = chain(src, mine, p.in_plane(left))
    passed.add(src, mine, partner)
    yield
    a.wait_recv()
    first = where(left, 0, half)
    f = chain(first, first, p.in_plane(right))
    hand(left)
    b.wait_recv()
    second = where(right, half, half)
    g = chain(second, second, p.in_plane(left))
    hand(right)
    yield
    f.wait_recv()
    g.wait_recv()
    hand(p.xslot(2))
    yield
    passed.wait_recv()


def plane_direct(copies, p, src, where, rows):
    partner = p.in_plane(p.xslot(0, True))
    chain = Chain(copies, where(0, 0, (G - 1) * rows))
    passed = Batch(copies, where(0, 0, X * rows), chain.group)

    def hand(slot):
        block = where(slot, 0, rows)
        passed.add(block, block, partner)

    mine = where(p.slot, 0, rows)
    c, a, b = [chain(src, mine, p.in_plane(p.xslot(s))) for s in (2, 1, -1)]
    passed.add(src, mine, partner)
    yield
    a.wait_recv()
    hand(p.xslot(-1))
    b.wait_recv()
    hand(p.xslot(1))
    yield
    c.wait_recv()
    hand(p.xslot(2))
    yield
    passed.wait_recv()


def whole(ref, rows):
    return lambda slot, offset, count: ref.at[at(slot, rows, offset, count)]


def column_ring(copies, p, src, ref):
    def block(distance):
        return ref.at[at(place(distance), TOK)]

    up, down = p.in_column(p.zslot(1)), p.in_column(p.zslot(-1))
    chain = Chain(copies, ref.at[pl.ds(0, (Z - 1) * TOK)])
    u = chain(src, block(-1), up)
    d = chain(src, block(1), down)
    for step in range(1, Z // 2 + 1):
        yield
        u.wait_recv()
        if step < Z // 2:
            u = chain(block(-step), block(-step - 1), up)
        if step < Z // 2:
            d.wait_recv()
            if step < Z // 2 - 1:
                d = chain(block(step), block(step + 1), down)


def run(*rings):
    rings = list(rings)
    while rings:
        rings = [ring for ring in rings if next(ring, True) is None]


def plane_peers(p):
    return [p.in_plane(p.xslot(s, f)) for s in range(X) for f in (False, True) if s or f]


def column_peers(p):
    return [p.in_column(p.zslot(s)) for s in range(1, Z)]


def row_peers(p):
    return [{"fsdp": p.yslot(s)} for s in range(1, Y)]


def sum_squares(ref, chunk=64):
    width = ref.shape[1]

    def step(i, acc):
        block = ref[pl.ds(pl.multiple_of(i * chunk, chunk), chunk), :].astype(F32)
        return acc + jnp.sum((block * block).reshape(chunk // 8, 8, width), axis=0)

    acc = lax.fori_loop(0, ref.shape[0] // chunk, step, jnp.zeros((8, width), F32))
    return jnp.sum(acc, axis=0, keepdims=True)


def place(distance):
    return ORDER.index(distance % Z)


def sum_squares(ref, chunk=64):
    width = ref.shape[1]

    def step(i, acc):
        block = ref[pl.ds(pl.multiple_of(i * chunk, chunk), chunk), :].astype(F32)
        return acc + jnp.sum((block * block).reshape(chunk // 8, 8, width), axis=0)

    acc = lax.fori_loop(0, ref.shape[0] // chunk, step, jnp.zeros((8, width), F32))
    return jnp.sum(acc, axis=0, keepdims=True)


def build_bias(owners, pos, bias, p):
    lane = lax.broadcasted_iota(jnp.int32, (1, TOK), 1)
    low = lane < HALF
    row = lax.broadcasted_iota(jnp.int32, (HALF, TOK), 0)

    def step(slot, carry):
        owner = owners[p.z * G + slot]
        where = lane + jnp.where(low, owner * HALF, (2 * PAIRS - 1 - owner) * HALF - HALF)
        floor = where - pos[slot, 0:1, :]
        cols = pl.ds(pl.multiple_of(slot * TOK, TOK), TOK)
        for distance in range(Z):
            owner = owners[p.zslot(distance) * G + p.slot]
            for h, stretch in enumerate((owner, 2 * PAIRS - 1 - owner)):
                key = row + stretch * HALF
                seen = (key <= where) & (key >= floor)
                rows = pl.ds(place(distance) * TOK + h * HALF, HALF)
                bias[rows, cols] = jnp.where(seen, 0.0, NEGATIVE)
        return carry

    lax.fori_loop(0, G, step, 0)


def tile_of(t):
    return pl.ds(pl.multiple_of(t * TILE, TILE), TILE)


def head_of(t, h):
    return pl.ds(pl.multiple_of((t * HEADS + h) * TILE, TILE), TILE)


def tile_stats(qg, dog, kg, vg, bias, masses, dps, tops, out, t):
    tile = tile_of(t)
    for h in range(HEADS):
        cols = pl.ds(h * DH, DH)
        raw = lax.dot_general(kg[...], qg[tile, cols], LAST, preferred_element_type=F32)
        raw = raw + bias[:, tile]
        top = jnp.max(raw, axis=0, keepdims=True)
        mass = jnp.exp2((raw - top) * SCALE2)
        total = jnp.sum(mass, axis=0, keepdims=True)
        masses[:, head_of(t, h)] = mass.astype(BF16)
        dp = lax.dot_general(vg[...], dog[tile, cols], LAST, preferred_element_type=F32)
        dps[:, head_of(t, h)] = dp
        dsum = jnp.sum(mass * dp, axis=0, keepdims=True)
        tops[h : h + 1, tile] = top * SCALE2
        out[h : h + 1, tile] = top * SCALE2 + jnp.log2(total)
        out[HEADS + h : HEADS + h + 1, tile] = dsum / total


def merge_stats(shared, tops, merged, t):
    tile = tile_of(t)
    for h in range(HEADS):
        parts = shared[:, h, tile]
        top = jnp.max(parts, axis=0, keepdims=True)
        weight = jnp.exp2(parts - top)
        total = jnp.sum(weight, axis=0, keepdims=True)
        merged[h : h + 1, tile] = jnp.exp2(tops[h : h + 1, tile] - (top + jnp.log2(total)))
        dsum = jnp.sum(weight * shared[:, HEADS + h, tile], axis=0, keepdims=True)
        merged[HEADS + h : HEADS + h + 1, tile] = dsum / total


def chunk_grads(
    qg, dog, kt, masses, dps, merged, probs, slopes, acc, dqt, dq, dk, dv, chunk, ready
):
    count = masses.shape[0] // CHUNKS
    rows = pl.ds(chunk * count, count)
    acc[...] = jnp.zeros_like(acc)

    def step(t, carry):
        ready(t)
        tile = tile_of(t)
        for h in range(HEADS):
            cols = pl.ds(h * DH, DH)
            wide = pl.ds(h * TILE, TILE)
            prob = masses[rows, head_of(t, h)].astype(F32) * merged[h : h + 1, tile]
            slope = prob * (dps[rows, head_of(t, h)] - merged[HEADS + h : HEADS + h + 1, tile])
            probs[:, wide] = prob.astype(BF16)
            slopes[:, wide] = slope.astype(BF16)
            part = jnp.dot(kt[:, rows], slopes[:, wide], preferred_element_type=F32)
            if chunk > 0:
                part = part + dqt[t, :, wide]
            if chunk < CHUNKS - 1:
                dqt[t, :, wide] = part
            else:
                dq[tile, cols] = (part * SCALE).T.astype(BF16)
        tall = lambda ref: jnp.concatenate(
            [ref[tile, pl.ds(h * DH, DH)] for h in range(HEADS)], axis=0
        )
        acc[:, :DH] += jnp.dot(slopes[...], tall(qg), preferred_element_type=F32)
        acc[:, DH:] += jnp.dot(probs[...], tall(dog), preferred_element_type=F32)
        return carry

    lax.fori_loop(0, qg.shape[0] // TILE, step, 0)
    dk[rows, :] = (acc[:, :DH] * SCALE).astype(BF16)
    dv[rows, :] = acc[:, DH:].astype(BF16)


FARTHEST = (4, 3, 5, 2, 6, 1, 7)


def rounded_sum(ref, i, count):
    total = ref[i, 0].astype(F32)
    for n in range(1, count):
        total = total + ref[i, n].astype(F32)
    return total.astype(BF16)


def kernel(
    owners, q, do, k, v, pos, hid, kw, vw, dq_slots, raw_k, raw_v, sums,
    qg, dog, kg, vg, pg, bias, shared, merged, kt, masses, dps, tops, probs, slopes, acc, dqt, dq, dk, dv,
    hg, hgt, pq, cq, gz, gy, grads, part, rz, ysum, wsum, tw, block, tot,
    send, recv, share_send, share_recv, local,
):
    p = Place()
    group = lax.div(p.y * HEADS, HPG)
    head_cols = pl.ds(pl.multiple_of(group * DH, DH), DH)
    own_k, own_v = k.at[:, head_cols], v.at[:, head_cols]
    wide = hid.shape[1] // G
    piece = wide // Z
    mine = at(p.slot, TOK)
    members = Y // KVG

    def strip(slot):
        return hid.at[:, pl.ds(pl.multiple_of(slot * wide, 128), wide)]

    moves = [
        (q, qg.at[mine]),
        (do, dog.at[mine]),
        (own_k, kg.at[at(place(0), TOK)]),
        (own_v, vg.at[at(place(0), TOK)]),
        (strip(p.slot), hg.at[mine]),
        (kw, tw.at[0]),
        (vw, tw.at[1]),
    ]
    everyone = plane_peers(p) + column_peers(p) + row_peers(p)
    greet(everyone)
    loads = [pltpu.make_async_copy(s, d, local.at[i]) for i, (s, d) in enumerate(moves)]
    for load in loads[5:] + loads[:5]:
        load.start()
    pg[p.slot] = jnp.broadcast_to(pos[...], (8, TOK))
    for i in range(2):
        loads[5 + i].wait()
        wsum[i] = jnp.broadcast_to(sum_squares(tw.at[i]), wsum.shape[1:])
    meet(everyone)
    copies = Copies(send, recv)
    small = Batch(copies, pg.at[pl.ds(0, G - 1)])
    for peer in plane_peers(p):
        small.add(pg.at[p.slot], pg.at[p.slot], peer)
    kr = column_ring(copies, p, own_k, kg)
    vr = column_ring(copies, p, own_v, vg)
    qr = plane_direct(copies, p, q, whole(qg, TOK), TOK)
    dr = plane_direct(copies, p, do, whole(dog, TOK), TOK)
    for ring in (kr, vr, qr, dr):
        next(ring)
    for ring in (kr, vr, kr, vr):
        next(ring)
    small.wait_recv()
    build_bias(owners, pg, bias, p)
    for ring in (kr, vr, qr, kr, vr, dr, qr, dr):
        next(ring, None)
    run(qr, dr)
    hs = Batch(copies, hg.at[pl.ds(0, (G - 1) * TOK)])
    for s, f in ((2, False), (2, True), (1, False), (3, False), (1, True), (3, True), (0, True)):
        to = p.xslot(s, f)
        hs.add(strip(to), hg.at[mine], p.in_plane(to))
    for load in loads[:5]:
        load.wait()
    kt[...] = kg[...].T
    peers = plane_peers(p)
    mine_stats = shared.at[p.slot]

    def share(t):
        block = shared.at[p.slot, :, tile_of(t)]
        return [
            pltpu.make_async_remote_copy(
                src_ref=block,
                dst_ref=block,
                send_sem=share_send.at[0],
                recv_sem=share_recv.at[t],
                device_id=peer,
                device_id_type=MESH,
            )
            for peer in peers
        ]

    def stats_step(t, carry):
        tile_stats(qg, dog, kg, vg, bias, masses, dps, tops, mine_stats, t)
        for copy in share(t):
            copy.start()
        return carry

    tiles = qg.shape[0] // TILE
    lax.fori_loop(0, tiles, stats_step, 0)

    def ready(t):
        take(shared.at[pl.ds(0, G - 1), :, tile_of(t)], share_recv.at[t])
        merge_stats(shared, tops, merged, t)

    scattered = [Batch(copies, gz.at[i, pl.ds(0, Z - 1)]) for i in range(2)]

    def scatter(chunk):
        count = Z // CHUNKS
        for i, src in enumerate((dk, dv)):
            for s in FARTHEST:
                if place(s) // count == chunk:
                    scattered[i].add(
                        src.at[at(place(s), TOK)], gz.at[i, p.z], p.in_column(p.zslot(s))
                    )

    for chunk in range(CHUNKS):
        chunk_grads(
            qg, dog, kt, masses, dps, merged, probs, slopes, acc, dqt, dq, dk, dv, chunk,
            ready if chunk == 0 else lambda t: None,
        )
        scatter(chunk)
    own_g = [
        pltpu.make_async_copy(src.at[at(place(0), TOK)], gz.at[i, p.z], local.at[7 + i])
        for i, src in enumerate((dk, dv))
    ]
    for load in own_g:
        load.start()

    def stream(i, raw):
        own_g[i].wait()
        scattered[i].wait_recv()
        gy[i, p.y] = rounded_sum(gz, i, Z)
        made = Batch(copies, gy.at[i, pl.ds(0, Y - 1)])
        for peer in row_peers(p):
            made.add(gy.at[i, p.y], gy.at[i, p.y], peer)
        yield
        made.wait_recv()
        for g in range(KVG):
            total = gy[i, g * members].astype(F32)
            for n in range(1, members):
                total = total + gy[i, g * members + n].astype(F32)
            grads[i, mine, g * DH : (g + 1) * DH] = total.astype(BF16)
        ring = plane_direct(copies, p, grads.at[i, mine], whole(grads.at[i], TOK), TOK)
        for _ in ring:
            yield
        product = jnp.dot(hgt[...], grads[i], preferred_element_type=F32)
        part[i] = product.astype(BF16)
        rz[i, p.z] = part[i, at(p.z, piece), :]
        made = Batch(copies, rz.at[i, pl.ds(0, Z - 1)])
        for s in FARTHEST:
            made.add(part.at[i, at(p.zslot(s), piece)], rz.at[i, p.z], p.in_column(p.zslot(s)))
        yield
        made.wait_recv()
        own = at(p.z, piece)
        block[i, own, :] = rounded_sum(rz, i, Z)
        made = Batch(copies, block.at[i, pl.ds(0, (Z - 1) * piece)])
        for s in FARTHEST:
            made.add(block.at[i, own], block.at[i, own], p.in_column(p.zslot(s)))
        yield
        made.wait_recv()
        ring = plane_ring(copies, p, block.at[i], whole(raw, wide), wide)
        next(ring)
        puts = [
            pltpu.make_async_copy(block.at[i], raw.at[at(p.slot, wide)], local.at[9 + i]),
            pltpu.make_async_copy(tot.at[i], sums.at[i, p.slot], local.at[11 + i]),
        ]
        puts[0].start()
        square = sum_squares(block.at[i])
        row = lax.broadcasted_iota(jnp.int32, (8, square.shape[1]), 0)
        ysum[i, p.y] = jnp.where(row == 0, square, wsum[i])
        made = Batch(copies, ysum.at[i, pl.ds(0, Y - 1)])
        for peer in row_peers(p):
            made.add(ysum.at[i, p.y], ysum.at[i, p.y], peer)
        yield
        next(ring)
        made.wait_recv()
        total = ysum[i, 0]
        for n in range(1, Y):
            total = total + ysum[i, n]
        tot[i] = total
        puts[1].start()
        made = Batch(copies, sums.at[i, pl.ds(0, G - 1)])
        for peer in plane_peers(p):
            made.add(tot.at[i], sums.at[i, p.slot], peer)
        yield
        next(ring)
        yield
        for _ in ring:
            pass
        made.wait_recv()
        for put in puts:
            put.wait()

    partner = p.in_plane(p.xslot(0, True))
    given = Batch(copies, pq)
    for x in range(X):
        given.add(dq.at[at(x * C + 1 - p.c, TOK)], pq.at[x], partner)
    hs.wait_recv()
    hgt[...] = hg[...].T
    streams = [stream(0, raw_k), stream(1, raw_v)]
    for one in streams:
        next(one)
    given.wait_recv()
    for x in range(X):
        cq[x] = (dq[at(x * C + p.c, TOK), :].astype(F32) + pq[x].astype(F32)).astype(BF16)
    put_q = pltpu.make_async_copy(cq.at[p.x], dq_slots.at[p.x], local.at[13])
    put_q.start()
    for _ in range(3):
        for one in streams:
            next(one)
    qs = Batch(copies, dq_slots.at[pl.ds(0, X - 1)])
    for s in (2, 1, 3):
        to = lax.rem(p.x + s, X)
        qs.add(cq.at[to], dq_slots.at[p.x], p.in_plane(to * C + p.c))
    run(*streams)
    qs.wait_recv()
    put_q.wait()
    copies.wait_sends()
    take(shared.at[pl.ds(0, G - 1)], share_send.at[0])


def shape(dims, kind=BF16):
    return jax.ShapeDtypeStruct(dims, kind)


def dma(n):
    return pltpu.SemaphoreType.DMA((n,))


def local(
    queries, keys, values, out_grad, hidden, key_weight, value_weight, stretch_owner, positions
):
    width = queries.shape[1]
    model = hidden.shape[1]
    piece = model // G
    columns = KVG * DH
    dq_slots, raw_k, raw_v, sums = pl.pallas_call(
        kernel,
        out_shape=(
            pltpu.VMEM((X, TOK, width), BF16),
            pltpu.VMEM((model, columns), BF16),
            pltpu.VMEM((model, columns), BF16),
            pltpu.VMEM((2, G, 8, columns), F32),
        ),
        in_specs=[SMEM] + [ANY] * 4 + [VMEM] + [ANY] * 3,
        out_specs=(ANY,) * 4,
        scratch_shapes=[
            pltpu.VMEM((ROWS, width), BF16),
            pltpu.VMEM((ROWS, width), BF16),
            pltpu.VMEM((Z * TOK, DH), BF16),
            pltpu.VMEM((Z * TOK, DH), BF16),
            pltpu.VMEM((G, 8, TOK), jnp.int32),
            pltpu.VMEM((Z * TOK, ROWS), F32),
            pltpu.VMEM((G, 2 * HEADS, ROWS), F32),
            pltpu.VMEM((2 * HEADS, ROWS), F32),
            pltpu.VMEM((DH, Z * TOK), BF16),
            pltpu.VMEM((Z * TOK, HEADS * ROWS), BF16),
            pltpu.VMEM((Z * TOK, HEADS * ROWS), F32),
            pltpu.VMEM((8, ROWS), F32),
            pltpu.VMEM((Z * TOK // CHUNKS, HEADS * TILE), BF16),
            pltpu.VMEM((Z * TOK // CHUNKS, HEADS * TILE), BF16),
            pltpu.VMEM((Z * TOK // CHUNKS, 2 * DH), F32),
            pltpu.VMEM((ROWS // TILE, DH, HEADS * TILE), F32),
            pltpu.VMEM((ROWS, width), BF16),
            pltpu.VMEM((Z * TOK, DH), BF16),
            pltpu.VMEM((Z * TOK, DH), BF16),
            pltpu.VMEM((ROWS, piece), BF16),
            pltpu.VMEM((piece, ROWS), BF16),
            pltpu.VMEM((X, TOK, width), BF16),
            pltpu.VMEM((X, TOK, width), BF16),
            pltpu.VMEM((2, Z, TOK, DH), BF16),
            pltpu.VMEM((2, Y, TOK, DH), BF16),
            pltpu.VMEM((2, ROWS, columns), BF16),
            pltpu.VMEM((2, piece, columns), BF16),
            pltpu.VMEM((2, Z, piece // Z, columns), BF16),
            pltpu.VMEM((2, Y, 8, columns), F32),
            pltpu.VMEM((2, 8, columns), F32),
            pltpu.VMEM((2, model, columns), BF16),
            pltpu.VMEM((2, piece, columns), BF16),
            pltpu.VMEM((2, 8, columns), F32),
            dma(SENDS),
            dma(RECVS),
            dma(1),
            dma(ROWS // TILE),
            dma(14),
        ],
        compiler_params=pltpu.CompilerParams(
            collective_id=0,
            has_side_effects=True,
            vmem_limit_bytes=VMEM_BYTES,
        ),
    )(
        stretch_owner, queries, out_grad, keys, values, positions.reshape(1, TOK),
        hidden, key_weight, value_weight,
    )
    query_grad = jnp.sum(dq_slots.astype(F32), axis=0).astype(BF16)
    tokens = TOK * PAIRS

    def clipped(i, raw):
        grad_norm = jnp.sqrt(jnp.sum(sums[i, :, 0], axis=0) + EPSILON)
        weight_norm = jnp.sqrt(sums[i, 0, 1] + EPSILON)
        factor = jnp.minimum(1.0, CLIP_RATE * tokens * weight_norm / grad_norm)
        return raw.astype(F32) * factor[None, :]

    return (query_grad, clipped(0, raw_k), clipped(1, raw_v))


def solution(mesh):
    return jax.shard_map(
        local,
        mesh=mesh,
        in_specs=(
            P("ctx", "fsdp"),
            P("ctx", None),
            P("ctx", None),
            P("ctx", "fsdp"),
            P("ctx", "fsdp"),
            P("fsdp", None),
            P("fsdp", None),
            P(),
            P("ctx"),
        ),
        out_specs=(P("ctx", "fsdp"), P("fsdp", None), P("fsdp", None)),
        check_vma=False,
    )
```
